512 devices in a mesh: dp: 32 (over y, x, core), table: 16 (over z).
Axes of the slice: x: 4, y: 4, z: 16, core: 2. Of those that a mesh axis runs over, the one named last changes fastest.
Arguments:
- hidden_in: bfloat16 [4096, 4096], P('dp', 'table'), may hold values from -6 to 6
- gate_weight: bfloat16 [4096, 4096], P('dp', 'table'), may hold values from -0.09375 to 0.09375
- values: bfloat16 [2048, 4096], P('table'), may hold values from -6 to 6
- pick_rows: int32 [4096, 32], P('dp'), may hold values from 0 to 2047, all different within a row
- pick_scores: float32 [4096, 32], P('dp'), may hold values from -300 to 300
- grad_out: bfloat16 [4096, 4096], P('dp', 'table'), may hold values from -6 to 6
Outputs:
- branch_out: bfloat16 [4096, 4096], P('dp', 'table')
- grad_hidden: bfloat16 [4096, 4096], P('dp', 'table')
- grad_gate: float32 [4096, 4096], P('dp', 'table')
- grad_values: float32 [2048, 4096], P('table')
- grad_scores: float32 [4096, 32], P('dp')
The draws below stay inside these ranges and needn't reach their ends.
Inputs may be any that keep to these rules, and one draw needn't show every extreme that they name: `pick_rows`: the 32 rows of a token are distinct.
All inputs are finite; a program needn't handle non-finite values.
Results may differ from the reference program's by a relative error of at most 0.025.
Values may be sent and summed in bfloat16 or wider, within the bound.
A program may use at most 64 MiB of HBM per device.

```python
import jax
import jax.numpy as jnp
from jax import lax

D = 4096
K = 32
TOK_DEV = 128
TOKENS = 4096
ROWS = 2048
N_DP = 32
N_TABLE = 16


def draw_pick_scores(key, part):
    first = jax.random.fold_in(key, 0)
    return jnp.clip(2.5 * jax.random.normal(first, (TOKENS, K), jnp.float32), -15.0, 15.0)


def levels(own_key, shape, shards, least, high):
    level = 1.0
    for position, shards_of in shards:
        heights = jax.random.uniform(jax.random.fold_in(jax.random.fold_in(own_key, 6), position), (shards_of,), jnp.float32, least / len(shards), high / len(shards))
        level = level * jnp.repeat(jnp.exp(heights), shape[position] // shards_of).reshape((-1,) + (1,) * (len(shape) - 1 - position))
    return level


def picks_of(rng, rows, amount, top, lift):
    sequence = jax.random.permutation(jax.random.fold_in(rng, 1), amount)
    pull = sequence
    for power in range(3):
        pull = pull * pull // amount
    pull = pull * lift // amount
    lots = jax.random.randint(jax.random.fold_in(rng, 2), (rows, amount), 0, 4096) + pull
    sure = jax.random.permutation(jax.random.fold_in(rng, 3), rows)[jnp.arange(amount) % rows]
    lots = jnp.where(jnp.arange(rows)[:, None] == sure[None, :], 1 << 14, lots)
    score = lots * amount + jnp.arange(amount)
    return lax.top_k(score.astype(jnp.int32), top)[1].astype(jnp.int32)


def normal_values(stream_key, shape, deviation, bound, cuts=(), held_as=jnp.bfloat16):
    level = levels(stream_key, shape, cuts, -0.22, 0.18) if cuts else 1.0
    array = jax.random.normal(stream_key, shape, jnp.float32) * deviation * level
    return jnp.minimum(jnp.maximum(array, -bound), bound).astype(held_as)


def setup_inputs(seed: int = 0) -> dict:
    key_list = jax.random.split(jax.random.key(seed), 7)
    hidden_in = normal_values(key_list[0], (TOKENS, D), 1.0, 6.0, ((0, 32), (1, 16)))
    gate_weight = normal_values(key_list[1], (D, D), D ** -0.5, 0.09375, ((0, 32), (1, 16)))
    values = normal_values(key_list[2], (ROWS, D), 1.0, 6.0, ((0, 16),))
    pick_rows = picks_of(key_list[3], TOKENS, ROWS, K, 256)
    pick_scores = draw_pick_scores(jax.random.fold_in(key_list[6], 71), 0)
    grad_out = normal_values(key_list[5], (TOKENS, D), 1.0, 6.0, ((0, 32), (1, 16)))
    return dict(hidden_in=hidden_in, gate_weight=gate_weight, values=values, pick_rows=pick_rows, pick_scores=pick_scores, grad_out=grad_out)


def silu_parts(gate_input):
    sigmoid_v = jax.nn.sigmoid(gate_input)
    return gate_input * sigmoid_v, sigmoid_v * (1.0 + gate_input * (1.0 - sigmoid_v))


def reference(hidden_in, gate_weight, values, pick_rows, pick_scores, grad_out):
    row_max = jnp.max(pick_scores, axis=1, keepdims=True)
    exponent = jnp.exp(pick_scores - row_max)
    weights = exponent / jnp.sum(exponent, axis=1, keepdims=True)
    weights_bf = lax.optimization_barrier(weights.astype(jnp.bfloat16))
    weight_wide = weights_bf.astype(jnp.float32)
    row_blocks = pick_rows.reshape(N_DP, TOK_DEV, K)
    weight_blocks = weight_wide.reshape(N_DP, TOK_DEV, K)

    def read_block(block_args):
        row_ids, block_weights = block_args
        picked = values[row_ids].astype(jnp.float32)
        return jnp.einsum("tk,tkd->td", block_weights, picked)

    memory_read = lax.map(read_block, (row_blocks, weight_blocks)).reshape(TOKENS, D)
    gate_input = jnp.dot(hidden_in, gate_weight, preferred_element_type=jnp.float32)
    gate_value, gate_slope = silu_parts(gate_input)
    branch_out = (memory_read * gate_value).astype(jnp.bfloat16)
    upstream = grad_out.astype(jnp.float32)
    mem_grad = (upstream * gate_value).astype(jnp.bfloat16)
    gate_grad_in = (upstream * memory_read * gate_slope).astype(jnp.bfloat16)
    grad_blocks = mem_grad.reshape(N_DP, TOK_DEV, D)

    def affinity_block(block_args):
        row_ids, block_grads = block_args
        picked = values[row_ids].astype(jnp.float32)
        return jnp.einsum("tkd,td->tk", picked, block_grads.astype(jnp.float32))

    affinity = lax.map(affinity_block, (row_blocks, grad_blocks)).reshape(TOKENS, K)
    grad_scores = weights * (affinity - jnp.sum(weights * affinity, axis=1, keepdims=True))

    def value_step(running, block_args):
        row_ids, block_weights, block_grads = block_args
        spread = block_weights[:, :, None] * block_grads.astype(jnp.float32)[:, None, :]
        block_term = jax.ops.segment_sum(spread.reshape(TOK_DEV * K, D), row_ids.reshape(TOK_DEV * K), num_segments=ROWS)
        rounded = lax.optimization_barrier(block_term.astype(jnp.bfloat16))
        return running + rounded.astype(jnp.float32), None

    grad_values, leftover = lax.scan(value_step, jnp.zeros((ROWS, D), jnp.float32), (row_blocks, weight_blocks, grad_blocks))

    def gate_step(running, block_args):
        block_in, block_grad = block_args
        block_term = lax.dot_general(block_in, block_grad, (((0,), (0,)), ((), ())), preferred_element_type=jnp.float32)
        rounded = lax.optimization_barrier(block_term.astype(jnp.bfloat16))
        return running + rounded.astype(jnp.float32), None

    grad_gate, leftover = lax.scan(gate_step, jnp.zeros((D, D), jnp.float32), (hidden_in.reshape(N_DP, TOK_DEV, D), gate_grad_in.reshape(N_DP, TOK_DEV, D)))
    col_width = D // N_TABLE
    grad_cols = gate_grad_in.reshape(TOKENS, N_TABLE, col_width).transpose(1, 0, 2)
    weight_cols = gate_weight.reshape(D, N_TABLE, col_width).transpose(1, 0, 2)

    def input_step(running, block_args):
        block_grad, block_weight = block_args
        block_term = lax.dot_general(block_grad, block_weight, (((1,), (1,)), ((), ())), preferred_element_type=jnp.float32)
        rounded = lax.optimization_barrier(block_term.astype(jnp.bfloat16))
        return running + rounded.astype(jnp.float32), None

    input_sum, leftover = lax.scan(input_step, jnp.zeros((TOKENS, D), jnp.float32), (grad_cols, weight_cols))
    grad_hidden = input_sum.astype(jnp.bfloat16)
    return (branch_out, grad_hidden, grad_gate, grad_values, grad_scores)
```

```python
import functools
import heapq

import jax
import jax.numpy as jnp
from jax import lax
from jax.experimental import pallas as pl
from jax.experimental.pallas import tpu as pltpu
from jax.sharding import PartitionSpec as P

MESH_ID = pl.DeviceIdType.MESH
F32 = jnp.float32
BF = jnp.bfloat16
NX = 4
NY = 4
CHUNKS = 2
N_COPIES = 256
N_LOCAL = 16
NT = (((1,), (1,)), ((), ()))


def wrap(value, size):
    return lax.rem(value + size, size)


def mult(value, unit):
    return pl.multiple_of(value, unit)


def run_streams(streams):
    heap = []
    for order, stream in enumerate(streams):
        heapq.heappush(heap, (0.0, order, stream))
    while heap:
        when, order, stream = heapq.heappop(heap)
        try:
            due = next(stream)
        except StopIteration:
            continue
        heapq.heappush(heap, (due, order, stream))


def body(
    nz,
    hid_in, w_in, val_in, rows_in, score_in, go_in,
    bo_out, gh_out, gg_out, gv_out, gs_out,
    hid, wts, vals, spread, spread_t, go, gin, mg, gg, pad_a, pad_b, rel_t, wgt, idx,
    pterm, pr0, psum, pr_bundle, pr_piece,
    tterm, tr0, tsum, tr_row, tr_col, tr_piece, tfin, gvals,
    iterm, ri, affp, affr, affall, afft,
    send_sem, recv_sem, local_sem,
):
    rows_blk = hid_in.shape[0]
    cols = hid_in.shape[1]
    b = lax.axis_index("dp")
    z = lax.axis_index("table")
    c = lax.rem(b, 2)
    x = lax.rem(lax.div(b, 2), NX)
    y = lax.div(b, 2 * NX)
    s = 1 - 2 * c
    oc = 1 - c

    def dev(yy, xx, cc):
        return ((yy * NX + xx) * 2 + cc, z)

    def zdev(delta):
        return (b, wrap(z + delta, nz))

    def xdev(delta):
        return dev(y, wrap(x + delta, NX), c)

    def ydev(delta):
        return dev(wrap(y + delta, NY), x, c)

    partner = dev(y, x, oc)

    barrier = pltpu.get_barrier_semaphore()
    peers = [zdev(k) for k in range(1, nz)] + [xdev(1), xdev(-1), ydev(1), ydev(-1), partner]
    for peer in peers:
        pl.semaphore_signal(barrier, inc=1, device_id=peer, device_id_type=MESH_ID)

    local_count = [0]
    copy_count = [0]
    sent = []

    def lcopy(src, dst):
        i = local_count[0]
        local_count[0] += 1
        cp = pltpu.make_async_copy(src, dst, local_sem.at[i])
        cp.start()
        return cp

    def send(src, dst, peer, track=True):
        i = copy_count[0]
        copy_count[0] += 1
        cp = pltpu.make_async_remote_copy(
            src_ref=src, dst_ref=dst, send_sem=send_sem.at[i], recv_sem=recv_sem.at[i],
            device_id=peer, device_id_type=MESH_ID,
        )
        cp.start()
        if track:
            sent.append(cp)
        return cp

    own_w = lcopy(w_in, wts.at[y, x, c])
    own_h = lcopy(hid_in, hid.at[z])
    own_g = lcopy(go_in, go)

    ylow = lax.rem(y, 2)
    yhigh = lax.div(y, 2)

    pad_a[...] = jnp.zeros_like(pad_a)
    pad_b[...] = jnp.zeros_like(pad_b)
    pad_a[:, 0:32] = rows_in[...].astype(F32)
    pad_b[:, 0:32] = score_in[...]
    total_rows = nz * rows_blk

    def relative(row_f):
        shifted = row_f.astype(jnp.int32) + (total_rows - rows_blk * z)
        return jnp.where(shifted >= total_rows, shifted - total_rows, shifted)

    idx[...] = relative(pad_a[...])
    rel_t[...] = relative(pad_a[...].T[0:32, :])
    scores = pad_b[...].T[0:32, :]
    expo = jnp.exp(scores - jnp.max(scores, axis=0, keepdims=True))
    wgt[...] = expo / jnp.sum(expo, axis=0, keepdims=True)
    weights_bf = wgt[...].astype(BF).astype(F32)
    afft[...] = weights_bf

    def spread_block(i, carry):
        ids = lax.broadcasted_iota(jnp.int32, (rows_blk, rows_blk), 0) + i * rows_blk
        acc = jnp.zeros((rows_blk, rows_blk), F32)
        for k in range(32):
            acc = jnp.where(rel_t[k : k + 1, :] == ids, afft[k : k + 1, :], acc)
        spread_t[i] = acc.astype(BF)
        spread[:, pl.ds(mult(i * rows_blk, rows_blk), rows_blk)] = acc.T.astype(BF)
        return carry

    lax.fori_loop(0, nz, spread_block, 0)

    own_w.wait()
    own_h.wait()
    own_g.wait()
    pl.semaphore_wait(barrier, len(peers))

    def w_piece(yy, xx, cc, half):
        return wts.at[yy, xx, cc, :, pl.ds(128 * half, 128)]

    def w_row(yy, cc, half):
        return wts.at[yy, :, cc, :, pl.ds(128 * half, 128)]

    def w_col(xx, cc, half):
        return wts.at[:, xx, cc, :, pl.ds(128 * half, 128)]

    def jset(cc, half):
        return pl.ds(8 * (1 - cc) + 4 * half, 4)

    def hi(yy):
        return pl.ds(mult(128 * lax.div(yy, 2), 128), 128)

    def t_slices(buf):
        def piece(yy, xx, cc, half):
            return buf.at[jset(cc, half), lax.rem(yy, 2), xx, :, hi(yy)]

        def row(yy, cc, half):
            return buf.at[jset(cc, half), lax.rem(yy, 2), :, :, hi(yy)]

        def col(xx, cc, half):
            return buf.at[jset(cc, half), :, xx]

        return piece, row, col

    def plane_gather(slices, half, t0, small, large, done):
        piece, row, col = slices
        if half == 0:
            line = lambda p: piece(y, p, c, half)
            bundle = lambda p, cc: row(p, cc, half)
            pos, near, pos2, near2, n1, n2 = x, xdev, y, ydev, NX, NY
        else:
            line = lambda p: piece(p, x, c, half)
            bundle = lambda p, cc: col(p, cc, half)
            pos, near, pos2, near2, n1, n2 = y, ydev, x, xdev, NY, NX
        up = send(line(pos), line(pos), near(1))
        down = send(line(pos), line(pos), near(-1))
        t = t0 + small
        yield t
        up.wait_recv()
        down.wait_recv()
        back = wrap(pos - s, n1)
        far = send(line(back), line(back), near(s))
        t += small
        yield t
        far.wait_recv()
        ups = send(bundle(pos2, c), bundle(pos2, c), near2(1))
        downs = send(bundle(pos2, c), bundle(pos2, c), near2(-1))
        swap = [send(bundle(pos2, c), bundle(pos2, c), partner)]
        t += large
        yield t
        ups.wait_recv()
        downs.wait_recv()
        back2 = wrap(pos2 - s, n2)
        fars = send(bundle(back2, c), bundle(back2, c), near2(s))
        for step in (-1, 1):
            p = wrap(pos2 + step, n2)
            swap.append(send(bundle(p, c), bundle(p, c), partner))
        t += large
        yield t
        fars.wait_recv()
        p = wrap(pos2 + 2, n2)
        swap.append(send(bundle(p, c), bundle(p, c), partner))
        t += small
        yield t
        for cp in swap:
            cp.wait_recv()
        done()

    pending = []
    state = {"w": 0}
    first = [True]

    def accumulate(block):
        q = wrap(z + block, nz)
        part = jnp.dot(
            hid[q], wts[lax.div(q, NX), lax.rem(q, NX)].reshape(cols, cols), preferred_element_type=F32
        )
        if first[0]:
            gin[...] = part
            first[0] = False
        else:
            gin[...] += part

    arrived = {}

    def block_here(block, parts):
        arrived[block] = arrived.get(block, 0) + parts
        if arrived[block] == CHUNKS:
            if state["w"] == 2:
                accumulate(block)
            else:
                pending.append(block)

    def w_done():
        state["w"] += 1
        if state["w"] == 2:
            for block in pending:
                accumulate(block)
            pending.clear()

    span = rows_blk // CHUNKS

    def hid_chunk(block, ch):
        return hid.at[wrap(z + block, nz), pl.ds(span * ch, span), :]

    def hid_ring(t0, step_time):
        flying = []
        for ch in range(CHUNKS):
            up_hops = nz // 2 if ch % 2 == 0 else nz // 2 - 1
            for sign, hops in ((1, up_hops), (-1, nz - 1 - up_hops)):
                cp = send(hid_chunk(0, ch), hid_chunk(0, ch), zdev(sign))
                flying.append([ch, sign, hops, 1, cp])
        block_here(0, CHUNKS)
        t = t0
        while flying:
            t += step_time
            yield t
            landed = []
            for item in list(flying):
                ch, sign, hops, k, cp = item
                cp.wait_recv()
                block = -sign * k
                landed.append(block % nz)
                if k < hops:
                    item[4] = send(hid_chunk(block, ch), hid_chunk(block, ch), zdev(sign))
                    item[3] = k + 1
                else:
                    flying.remove(item)
            for block in landed:
                block_here(block, 1)

    def tile_exchange(make_src, make_dst, toward):
        cps = []
        for i in range(1, nz // 2):
            j = jnp.where(c == 0, nz - i, i)
            cps.append(send(make_src(j), make_dst(j), (b, wrap(z + toward(j), nz))))
        half = nz // 2
        i = copy_count[0]
        copy_count[0] += 1
        last = pltpu.make_async_remote_copy(
            src_ref=make_src(half), dst_ref=make_dst(half), send_sem=send_sem.at[i], recv_sem=recv_sem.at[i],
            device_id=zdev(half), device_id_type=MESH_ID,
        )
        i = local_count[0]
        local_count[0] += 1
        own = pltpu.make_async_copy(make_src(0), make_dst(0), local_sem.at[i])

        @pl.when(c == 0)
        def _():
            last.start()

        @pl.when(c == 1)
        def _():
            own.start()

        def finish():
            for cp in cps:
                cp.wait_recv()

            @pl.when(c == 0)
            def _():
                last.wait()

            @pl.when(c == 1)
            def _():
                own.wait()

        return finish

    v_slices = t_slices(vals)
    tile_rows = lax.rem(y, 2) * NX + x

    def val_src(j):
        zd = wrap(z - j, nz)
        return val_in.at[pl.ds(mult(16 * tile_rows, 16), 16), pl.ds(mult(cols * zd + 128 * yhigh, 128), 128)]

    def val_dst(j):
        return vals.at[j, ylow, x, :, hi(y)]

    def both(make):
        parts = [make(half) for half in (0, 1)]
        live = list(parts)
        while live:
            due = None
            for part in list(live):
                try:
                    due = next(part)
                except StopIteration:
                    live.remove(part)
            if live:
                yield due

    def v_path():
        yield 0.01
        finish = tile_exchange(val_src, val_dst, lambda j: nz - j)
        yield 8.0
        finish()
        yield from both(lambda half: plane_gather(v_slices, half, 8.0, 2.2, 3.0, lambda: None))

    w_slices = (w_piece, w_row, w_col)
    run_streams(
        [
            hid_ring(0.0, 2.4),
            v_path(),
            both(lambda half: plane_gather(w_slices, half, 0.0, 2.3, 4.0, w_done)),
        ]
    )

    gate = gin[...]
    sig = jax.nn.sigmoid(gate)
    gate_value = gate * sig
    upstream = go[...].astype(F32)
    mg[...] = (upstream * gate_value).astype(BF)

    t_swap = []
    for owner in (oc, c):
        for jl in range(8):
            j = 8 * (1 - owner) + jl
            tterm[j] = jnp.dot(spread_t[j], mg[...], preferred_element_type=F32).astype(BF).reshape(2, NX, 16, cols)
        if not t_swap:
            t_swap = [send(tterm.at[jset(oc, h)], tr0.at[pl.ds(4 * h, 4)], partner) for h in (0, 1)]

    memory_read = jnp.dot(spread[...], vals[...].reshape(total_rows, cols), preferred_element_type=F32)
    bo_out[...] = (memory_read * gate_value).astype(BF)
    gg_f = (upstream * memory_read * (sig * (1.0 + gate * (1.0 - sig)))).astype(BF)
    gg[...] = gg_f
    ggt = gg_f.astype(F32).T.astype(BF)

    def make_iterm(block):
        q = wrap(z + block, nz)
        iterm[q] = lax.dot_general(
            gg[...], wts[lax.div(q, NX), lax.rem(q, NX)].reshape(cols, cols), NT, preferred_element_type=F32
        ).astype(BF)

    made = set()

    def need_iterm(block):
        if block % nz not in made:
            made.add(block % nz)
            make_iterm(block)

    def i_chunk(block, ch):
        return iterm.at[wrap(z + block, nz), pl.ds(span * ch, span), :]

    def hidden_ring(t0, step_time):
        flying = []
        for ch in range(CHUNKS):
            up_hops = nz // 2 if ch % 2 == 0 else nz // 2 - 1
            for sign, hops in ((1, up_hops), (-1, nz - 1 - up_hops)):
                need_iterm(sign * hops)
                slot = ri.at[(1 - sign) // 2, 0, pl.ds(span * ch, span), :]
                cp = send(i_chunk(sign * hops, ch), slot, zdev(sign))
                flying.append([ch, sign, hops, 1, cp])
        t = t0
        while flying:
            for item in flying:
                ch, sign, hops, k, cp = item
                if k < hops:
                    need_iterm(sign * (hops - k))
            t += step_time
            yield t
            for item in list(flying):
                ch, sign, hops, k, cp = item
                cp.wait_recv()
                if k < hops:
                    block = sign * (hops - k)
                    q = wrap(z + block, nz)
                    here = pl.ds(span * ch, span)
                    total = iterm[q, here, :].astype(F32) + ri[(1 - sign) // 2, k - 1, here, :].astype(F32)
                    iterm[q, here, :] = total.astype(BF)
                    slot = ri.at[(1 - sign) // 2, k, here, :]
                    item[4] = send(i_chunk(block, ch), slot, zdev(sign))
                    item[3] = k + 1
                else:
                    flying.remove(item)
        need_iterm(0)
        for ch in range(CHUNKS):
            up_hops = nz // 2 if ch % 2 == 0 else nz // 2 - 1
            here = pl.ds(span * ch, span)
            total = iterm[z, here, :].astype(F32)
            total = total + ri[0, up_hops - 1, here, :].astype(F32) + ri[1, nz - 2 - up_hops, here, :].astype(F32)
            gh_out[here, :] = total.astype(BF)

    def plane_reduce(slices, half, bufs, t0, small, large, finish):
        piece, row, col = slices
        rb, rp = bufs
        if half == 0:
            bundle = lambda p: row(p, half)
            line = lambda p: piece(y, p, half)
            pos, near, pos2, near2, n1, n2 = y, ydev, x, xdev, NY, NX
        else:
            bundle = lambda p: col(p, half)
            line = lambda p: piece(p, x, half)
            pos, near, pos2, near2, n1, n2 = x, xdev, y, ydev, NX, NY
        t = t0
        for stage, (at, p0, nr, n, rbuf, dt) in enumerate(
            ((bundle, pos, near, n1, rb, large), (line, pos2, near2, n2, rp, small))
        ):
            relay = send(at(wrap(p0 + 2, n)), rbuf.at[0], nr(s))
            direct = send(at(wrap(p0 - s, n)), rbuf.at[1], nr(-s))
            t += dt
            yield t
            relay.wait_recv()
            ahead = at(wrap(p0 + s, n))
            ahead[...] = (ahead[...].astype(F32) + rbuf[0].astype(F32)).astype(BF)
            comb = send(ahead, rbuf.at[2], nr(s))
            t += dt
            yield t
            direct.wait_recv()
            comb.wait_recv()
            mine = at(p0)
            total = mine[...].astype(F32) + rbuf[1].astype(F32) + rbuf[2].astype(F32)
            if stage == 0:
                mine[...] = total.astype(BF)
            else:
                finish(total)

    def ts_piece(yy, xx, half):
        return tsum.at[pl.ds(4 * half, 4), lax.rem(yy, 2), xx, :, hi(yy)]

    def ts_row(yy, half):
        return tsum.at[pl.ds(4 * half, 4), lax.rem(yy, 2), :, :, hi(yy)]

    def ts_col(xx, half):
        return tsum.at[pl.ds(4 * half, 4), :, xx]

    def g_src(j):
        jl = j - 8 * (1 - c)
        return tfin.at[jl]

    def g_src_fixed(j):
        return tfin.at[0] if isinstance(j, int) else g_src(j)

    def g_dst(j):
        return gvals.at[j, ylow, x, :, hi(y)]

    g_slices = t_slices(gvals)

    def t_half(half):
        yield 2.0
        t_swap[half].wait_recv()
        here = pl.ds(4 * half, 4)
        tsum[here] = (tterm[jset(c, half)].astype(F32) + tr0[here].astype(F32)).astype(BF)

        def finish(total):
            tfin[here] = total.astype(BF)

        yield from plane_reduce(
            (ts_piece, ts_row, ts_col), half, (tr_row if half == 0 else tr_col, tr_piece.at[half]),
            2.0, 2.2, 3.0, finish,
        )

    def t_path():
        yield from both(t_half)
        done = tile_exchange(g_src_fixed, g_dst, lambda j: j)
        yield 20.0
        done()
        yield from both(lambda half: plane_gather(g_slices, half, 20.0, 2.2, 3.0, lambda: None))
        for j in range(nz):
            q = wrap(z - j, nz)
            gv_out[:, pl.ds(mult(q * cols, cols), cols)] = gvals[j].reshape(rows_blk, cols).astype(F32)

    def ps_piece(yy, xx, half):
        return psum.at[yy, xx, pl.ds(128 * half, 128), :]

    def ps_row(yy, half):
        return psum.at[yy, :, pl.ds(128 * half, 128), :]

    def ps_col(xx, half):
        return psum.at[:, xx, pl.ds(128 * half, 128), :]

    def p_half(half):
        here = pl.ds(128 * half, 128)
        lhs = ggt[128 * half : 128 * half + 128, :]
        yield 0.5 + half
        for q in range(nz):
            pterm[q // NX, q % NX, here, :] = jnp.dot(lhs, hid[q], preferred_element_type=F32).astype(BF)
        swap = send(
            pterm.at[:, :, here, pl.ds(mult(128 * oc, 128), 128)], pr0.at[half], partner
        )
        yield 4.0 + half
        swap.wait_recv()
        own = pterm[:, :, here, pl.ds(mult(128 * c, 128), 128)]
        psum[:, :, here, :] = (own.astype(F32) + pr0[half].astype(F32)).astype(BF)

        def finish(total):
            gg_out[:, pl.ds(128 * half, 128)] = total.T

        yield from plane_reduce(
            (ps_piece, ps_row, ps_col), half, (pr_bundle.at[half], pr_piece.at[half]), 4.0 + half, 2.2, 4.5, finish
        )

    def aff_path():
        yield 3.0
        lane = jnp.bitwise_and(idx[...], 127)
        chunk = lax.shift_right_logical(idx[...], 7)
        acc = jnp.zeros((rows_blk, 128), F32)
        for j in range(nz):
            part = lax.dot_general(mg[...], vals[j].reshape(rows_blk, cols), NT, preferred_element_type=F32)
            got = jnp.take_along_axis(part, lane, axis=1, mode="promise_in_bounds")
            acc = jnp.where(chunk == j, got, acc)
        acc_t = acc.T
        for i in range(nz):
            affp[i] = acc_t[2 * i : 2 * i + 2, :]
        cps = [send(affp.at[wrap(z + k, nz)], affr.at[k], zdev(k)) for k in range(1, nz)]
        yield 13.0
        total = affp[z]
        for k in range(1, nz):
            cps[k - 1].wait_recv()
            total = total + affr[k]
        affall[z] = total
        cps = [send(affall.at[z], affall.at[z], zdev(k)) for k in range(1, nz)]
        yield 21.0
        for cp in cps:
            cp.wait_recv()
        for i in range(nz):
            afft[2 * i : 2 * i + 2, :] = affall[i]
        weights = wgt[...]
        aff = afft[...]
        pad_b[0:32, :] = weights * (aff - jnp.sum(weights * aff, axis=0, keepdims=True))
        gs_out[...] = pad_b[...].T[:, 0:32]

    run_streams([t_path(), hidden_ring(0.0, 2.5), p_half(0), p_half(1), aff_path()])

    for cp in sent:
        cp.wait_send()


def layer(nz, hidden_in, gate_weight, values, pick_rows, pick_scores, grad_out):
    rows, cols = hidden_in.shape
    vm = pltpu.VMEM
    scratch = [
        vm((nz, rows, cols), BF),
        vm((NY, NX, 2, rows, cols), BF),
        vm((nz, 2, NX, 16, cols), BF),
        vm((rows, nz * rows), BF),
        vm((nz, rows, rows), BF),
        vm((rows, cols), BF),
        vm((rows, cols), F32),
        vm((rows, cols), BF),
        vm((rows, cols), BF),
        vm((rows, 128), F32),
        vm((rows, 128), F32),
        vm((32, rows), jnp.int32),
        vm((32, rows), F32),
        vm((rows, 128), jnp.int32),
        vm((NY, NX, cols, cols), BF),
        vm((2, NY, NX, 128, 128), BF),
        vm((NY, NX, cols, 128), BF),
        vm((2, 3, 4, 128, 128), BF),
        vm((2, 3, 128, 128), BF),
        vm((nz, 2, NX, 16, cols), BF),
        vm((8, 2, NX, 16, cols), BF),
        vm((8, 2, NX, 16, cols), BF),
        vm((3, 4, NX, 16, 128), BF),
        vm((3, 4, 2, 16, cols), BF),
        vm((2, 3, 4, 16, 128), BF),
        vm((8, 16, 128), BF),
        vm((nz, 2, NX, 16, cols), BF),
        vm((nz, rows, cols), BF),
        vm((2, nz // 2, rows, cols), BF),
        vm((nz, 2, 128), F32),
        vm((nz, 2, 128), F32),
        vm((nz, 2, 128), F32),
        vm((32, 128), F32),
        pltpu.SemaphoreType.DMA((N_COPIES,)),
        pltpu.SemaphoreType.DMA((N_COPIES,)),
        pltpu.SemaphoreType.DMA((N_LOCAL,)),
    ]
    hbm = pl.BlockSpec(memory_space=pl.ANY)
    vmem = pl.BlockSpec(memory_space=pltpu.VMEM)
    return pl.pallas_call(
        functools.partial(body, nz),
        out_shape=(
            jax.ShapeDtypeStruct((rows, cols), BF),
            jax.ShapeDtypeStruct((rows, cols), BF),
            jax.ShapeDtypeStruct((rows, cols), F32),
            jax.ShapeDtypeStruct((rows, nz * cols), F32),
            jax.ShapeDtypeStruct((rows, 32), F32),
        ),
        in_specs=[hbm, hbm, hbm, vmem, vmem, hbm],
        out_specs=(vmem,) * 5,
        scratch_shapes=scratch,
        compiler_params=pltpu.CompilerParams(collective_id=0, has_side_effects=True),
    )(hidden_in, gate_weight, values, pick_rows, pick_scores, grad_out)


def solution(mesh):
    nz = mesh.shape["table"]
    return jax.shard_map(
        functools.partial(layer, nz),
        mesh=mesh,
        in_specs=(
            P("dp", "table"),
            P("dp", "table"),
            P("table", None),
            P("dp", None),
            P("dp", None),
            P("dp", "table"),
        ),
        out_specs=(
            P("dp", "table"),
            P("dp", "table"),
            P("dp", "table"),
            P("table", None),
            P("dp", None),
        ),
        check_vma=False,
    )
```

```python
import functools
import heapq

import jax
import jax.numpy as jnp
from jax import lax
from jax.experimental import pallas as pl
from jax.experimental.pallas import tpu as pltpu
from jax.sharding import PartitionSpec as P

MESH_ID = pl.DeviceIdType.MESH
F32 = jnp.float32
BF = jnp.bfloat16
NX = 4
NY = 4
CHUNKS = 2
N_COPIES = 256
N_LOCAL = 16
NT = (((1,), (1,)), ((), ()))


def wrap(value, size):
    return lax.rem(value + size, size)


def mult(value, unit):
    return pl.multiple_of(value, unit)


def run_streams(streams):
    heap = []
    for order, stream in enumerate(streams):
        heapq.heappush(heap, (0.0, order, stream))
    while heap:
        when, order, stream = heapq.heappop(heap)
        try:
            due = next(stream)
        except StopIteration:
            continue
        heapq.heappush(heap, (due, order, stream))


def body(
    nz,
    hid_in, w_in, val_in, rows_in, score_in, go_in,
    bo_out, gh_out, gg_out, gvals_out, gs_out,
    hid, wts, vals, spread, spread_t, go, gin, mg, gg, ggt, pad_a, picks, rel_t, wgt, idx,
    pterm, pr0, psum, pr_bundle, pr_piece,
    tterm, tr0, tsum, tr_row, tr_col, tr_piece, tfin, gvals,
    iterm, ri_even, ri_odd, affp, affr, affall, afft,
    send_sem, recv_sem, local_sem, know,
):
    rows_blk = hid_in.shape[0]
    cols = hid_in.shape[1]
    b = lax.axis_index("dp")
    z = lax.axis_index("table")
    c = lax.rem(b, 2)
    x = lax.rem(lax.div(b, 2), NX)
    y = lax.div(b, 2 * NX)
    s = 1 - 2 * c
    oc = 1 - c

    def dev(yy, xx, cc):
        return ((yy * NX + xx) * 2 + cc, z)

    def zdev(delta):
        return (b, wrap(z + delta, nz))

    def xdev(delta):
        return dev(y, wrap(x + delta, NX), c)

    def ydev(delta):
        return dev(wrap(y + delta, NY), x, c)

    partner = dev(y, x, oc)

    barrier = pltpu.get_barrier_semaphore()
    peers = [zdev(k) for k in (1, -1, 2, -2)] + [xdev(k) for k in (1, 2, 3)] + [ydev(k) for k in (1, 2, 3)]
    peers.append(partner)
    for peer in peers:
        pl.semaphore_signal(barrier, inc=1, device_id=peer, device_id_type=MESH_ID)

    local_count = [0]
    copy_count = [0]
    sent = []

    def lcopy(src, dst):
        i = local_count[0]
        local_count[0] += 1
        cp = pltpu.make_async_copy(src, dst, local_sem.at[i])
        cp.start()
        return cp

    def send(src, dst, peer):
        i = copy_count[0]
        copy_count[0] += 1
        cp = pltpu.make_async_remote_copy(
            src_ref=src, dst_ref=dst, send_sem=send_sem.at[i], recv_sem=recv_sem.at[i],
            device_id=peer, device_id_type=MESH_ID,
        )
        cp.start()
        sent.append(cp)
        return cp

    own_rows = lcopy(rows_in, picks)
    own_scores = lcopy(score_in, wgt)
    own_w = lcopy(w_in, wts.at[y, x, c])
    own_h = lcopy(hid_in, hid.at[z])
    own_g = lcopy(go_in, go)

    ylow = lax.rem(y, 2)
    yhigh = lax.div(y, 2)

    pad_a[...] = jnp.zeros_like(pad_a)
    own_rows.wait()
    own_scores.wait()
    pad_a[0:32, :] = picks[...].astype(F32)
    total_rows = nz * rows_blk

    def relative(row_f):
        shifted = row_f.astype(jnp.int32) + (total_rows - rows_blk * z)
        return jnp.where(shifted >= total_rows, shifted - total_rows, shifted)

    idx[...] = relative(pad_a[...].T)
    rel_t[...] = relative(pad_a[0:32, :])
    scores = wgt[...]
    expo = jnp.exp(scores - jnp.max(scores, axis=0, keepdims=True))
    wgt[...] = expo / jnp.sum(expo, axis=0, keepdims=True)
    weights_bf = wgt[...].astype(BF).astype(F32)
    afft[...] = weights_bf

    def spread_block(i, carry):
        ids = lax.broadcasted_iota(jnp.int32, (rows_blk, rows_blk), 0) + i * rows_blk
        acc = jnp.zeros((rows_blk, rows_blk), F32)
        for k in range(32):
            acc = jnp.where(rel_t[k : k + 1, :] == ids, afft[k : k + 1, :], acc)
        spread_t[i] = acc.astype(BF)
        spread[:, pl.ds(mult(i * rows_blk, rows_blk), rows_blk)] = acc.T.astype(BF)
        return carry

    own_w.wait()
    own_h.wait()
    own_g.wait()
    pl.semaphore_wait(barrier, len(peers))

    def w_piece(yy, xx, cc, half):
        return wts.at[yy, xx, cc, :, pl.ds(128 * half, 128)]

    def w_row(yy, cc, half):
        return wts.at[yy, :, cc, :, pl.ds(128 * half, 128)]

    def w_col(xx, cc, half):
        return wts.at[:, xx, cc, :, pl.ds(128 * half, 128)]

    def jset(cc, half):
        return pl.ds(8 * (1 - cc) + 4 * half, 4)

    def hi(yy):
        return pl.ds(mult(128 * lax.div(yy, 2), 128), 128)

    def t_slices(buf):
        def piece(yy, xx, cc, half):
            return buf.at[jset(cc, half), lax.rem(yy, 2), xx, :, hi(yy)]

        def row(yy, cc, half):
            return buf.at[jset(cc, half), lax.rem(yy, 2), :, :, hi(yy)]

        def col(xx, cc, half):
            return buf.at[jset(cc, half), :, xx]

        return piece, row, col

    flags = set()

    def until(name, t):
        while name not in flags:
            yield t
            t += 0.5

    def both(make):
        live = [make(half) for half in (0, 1)]
        while live:
            due = None
            for part in list(live):
                try:
                    due = next(part)
                except StopIteration:
                    live.remove(part)
            if live:
                yield due

    def plane_gather(slices, half, t, first_step, second_step, third_step):
        piece, row, col = slices
        if half == 0:
            line = lambda p: piece(y, p, c, half)
            bundle = lambda p: row(p, c, half)
            pos, near, pos2, near2, n1, n2 = x, xdev, y, ydev, NX, NY
        else:
            line = lambda p: piece(p, x, c, half)
            bundle = lambda p: col(p, c, half)
            pos, near, pos2, near2, n1, n2 = y, ydev, x, xdev, NY, NX
        out = [send(line(pos), line(pos), near(k)) for k in (2, 1, 3)]
        t += first_step
        yield t
        for cp in out:
            cp.wait_recv()
        out = [send(bundle(pos2), bundle(pos2), near2(k)) for k in (2, 1, 3)]
        swap = [send(bundle(pos2), bundle(pos2), partner)]
        t += second_step
        yield t
        for k, cp in ((1, out[1]), (3, out[2]), (2, out[0])):
            cp.wait_recv()
            p = wrap(pos2 - k, n2)
            swap.append(send(bundle(p), bundle(p), partner))
        t += third_step
        yield t
        for cp in swap:
            cp.wait_recv()

    pending = []
    first = [True]

    def accumulate(block):
        q = wrap(z + block, nz)
        part = jnp.dot(
            hid[q], wts[lax.div(q, NX), lax.rem(q, NX)].reshape(cols, cols), preferred_element_type=F32
        )
        if first[0]:
            gin[...] = part
            first[0] = False
        else:
            gin[...] += part

    arrived = {}

    def block_here(block, parts):
        arrived[block] = arrived.get(block, 0) + parts
        if arrived[block] == CHUNKS:
            if "w" in flags:
                accumulate(block)
            else:
                pending.append(block)

    span = rows_blk // CHUNKS

    def hid_chunk(block, ch):
        return hid.at[wrap(z + block, nz), pl.ds(span * ch, span), :]

    def limits(ch):
        up = nz // 2 if ch % 2 == 0 else nz // 2 - 1
        return ((1, up), (-1, nz - 1 - up))

    def hid_relay(t, step_time):
        def pass_on(ch, sign, limit, k):
            at = hid_chunk(-sign * k, ch)
            far = send(at, at, zdev(2 * sign)) if k + 2 <= limit else None
            near = send(at, at, zdev(sign)) if k + 1 <= limit else None
            return [ch, sign, limit, k, near, far]

        flying = [pass_on(ch, sign, limit, 0) for ch in range(CHUNKS) for sign, limit in limits(ch)]
        block_here(0, CHUNKS)
        lax.fori_loop(0, nz, spread_block, 0)
        while flying:
            t += step_time
            yield t
            following, landed = [], []
            for ch, sign, limit, k, near, far in flying:
                if far is not None:
                    far.wait_recv()
                    following.append(pass_on(ch, sign, limit, k + 2))
                    landed.append((-sign * (k + 2)) % nz)
                if near is not None:
                    near.wait_recv()
                    landed.append((-sign * (k + 1)) % nz)
            flying = following
            for block in landed:
                block_here(block, 1)
        yield from until("w", t)
        flags.add("h")

    def tile_exchange(make_src, make_dst, toward):
        cps = []
        for i in range(1, nz // 2):
            j = jnp.where(c == 0, nz - i, i)
            cps.append(send(make_src(j), make_dst(j), (b, wrap(z + toward(j), nz))))
        half = nz // 2
        i = copy_count[0]
        copy_count[0] += 1
        last = pltpu.make_async_remote_copy(
            src_ref=make_src(half), dst_ref=make_dst(half), send_sem=send_sem.at[i], recv_sem=recv_sem.at[i],
            device_id=zdev(half), device_id_type=MESH_ID,
        )
        i = local_count[0]
        local_count[0] += 1
        own = pltpu.make_async_copy(make_src(0), make_dst(0), local_sem.at[i])

        @pl.when(c == 0)
        def _():
            last.start()

        @pl.when(c == 1)
        def _():
            own.start()

        def finish():
            for cp in cps:
                cp.wait_recv()

            @pl.when(c == 0)
            def _():
                last.wait()

            @pl.when(c == 1)
            def _():
                own.wait()

        return finish

    v_slices = t_slices(vals)
    tile_rows = lax.rem(y, 2) * NX + x

    def val_src(j):
        zd = wrap(z - j, nz)
        return val_in.at[pl.ds(mult(16 * tile_rows, 16), 16), pl.ds(mult(cols * zd + 128 * yhigh, 128), 128)]

    def val_dst(j):
        return vals.at[j, ylow, x, :, hi(y)]

    def both(make):
        parts = [make(half) for half in (0, 1)]
        live = list(parts)
        while live:
            due = None
            for part in list(live):
                try:
                    due = next(part)
                except StopIteration:
                    live.remove(part)
            if live:
                yield due

    def v_path():
        yield 0.0
        for stage, reach in enumerate((2, 4)):
            for sign in (1, -1):
                pl.semaphore_signal(know.at[stage], inc=1, device_id=zdev(sign * reach), device_id_type=MESH_ID)
            yield (1.6, 4.5)[stage]
            pl.semaphore_wait(know.at[stage], 2)
        finish = tile_exchange(val_src, val_dst, lambda j: nz - j)
        yield 12.5
        finish()
        yield from both(lambda half: plane_gather(v_slices, half, 12.5, 3.4, 5.5, 1.5))
        flags.add("v")

    w_slices = (w_piece, w_row, w_col)

    def w_path():
        yield from both(lambda half: plane_gather(w_slices, half, 0.0, 3.5, 8.0, 1.7))
        flags.add("w")
        for block in pending:
            accumulate(block)
        pending.clear()

    def gate_parts():
        gate = gin[...]
        sig = jax.nn.sigmoid(gate)
        return gate, sig, go[...].astype(F32)

    t_swap = []

    def value_terms():
        gate, sig, upstream = gate_parts()
        mg[...] = (upstream * (gate * sig)).astype(BF)
        for owner in (oc, c):
            for jl in range(8):
                j = 8 * (1 - owner) + jl
                tterm[j] = (
                    jnp.dot(spread_t[j], mg[...], preferred_element_type=F32).astype(BF).reshape(2, NX, 16, cols)
                )
            if not t_swap:
                t_swap.extend(send(tterm.at[jset(oc, h)], tr0.at[pl.ds(4 * h, 4)], partner) for h in (0, 1))

    def gate_gradient():
        gate, sig, upstream = gate_parts()
        memory_read = jnp.dot(spread[...], vals[...].reshape(total_rows, cols), preferred_element_type=F32)
        bo_out[...] = (memory_read * (gate * sig)).astype(BF)
        slope = (upstream * memory_read * (sig * (1.0 + gate * (1.0 - sig)))).astype(BF)
        gg[...] = slope
        ggt[...] = slope.astype(F32).T.astype(BF)

    def make_iterm(block):
        q = wrap(z + block, nz)
        iterm[q] = lax.dot_general(
            gg[...], wts[lax.div(q, NX), lax.rem(q, NX)].reshape(cols, cols), NT, preferred_element_type=F32
        ).astype(BF)

    made = set()

    def need_iterm(block):
        if block % nz not in made:
            made.add(block % nz)
            make_iterm(block)

    def i_chunk(block, ch):
        return iterm.at[wrap(z + block, nz), pl.ds(span * ch, span), :]

    def slots(buf, sign, at, ch):
        return buf.at[(1 - sign) // 2, at, pl.ds(span * ch, span), :]

    def hidden_relay(t, step_time):
        yield from until("v", t)
        gate_gradient()
        flags.add("g")
        todo = [(ch, sign, limit) for ch in range(CHUNKS) for sign, limit in limits(ch)]
        far, near = {}, {}

        def start(ch, sign, dist, step):
            need_iterm(sign * dist)
            cps, buf = (far, ri_even) if step == 2 else (near, ri_odd)
            cps[ch, sign] = send(i_chunk(sign * dist, ch), slots(buf, sign, (dist - 1) // 2, ch), zdev(step * sign))

        for ch, sign, limit in todo:
            if limit == 8:
                start(ch, sign, 8, 2)
            start(ch, sign, 7, 1)
        for dist in (6, 4, 2, 0):
            for ch, sign, limit in todo:
                need_iterm(sign * dist)
                if dist:
                    need_iterm(sign * (dist - 1))
            t += step_time
            yield t
            for ch, sign, limit in todo:
                here = pl.ds(span * ch, span)
                side = (1 - sign) // 2
                q = wrap(z + sign * dist, nz)
                total = iterm[q, here, :].astype(F32)
                if (ch, sign) in far:
                    far[ch, sign].wait_recv()
                    total = total + ri_even[side, (dist + 1) // 2, here, :].astype(F32)
                near[ch, sign].wait_recv()
                total = total + ri_odd[side, dist // 2, here, :].astype(F32)
                if dist:
                    iterm[q, here, :] = total.astype(BF)
                    start(ch, sign, dist, 2)
                    start(ch, sign, dist - 1, 1)
                elif sign == limits(ch)[0][0]:
                    held = total
                    gin[here, :] = held
                else:
                    total = total - iterm[q, here, :].astype(F32) + gin[here, :]
                    gh_out[here, :] = total.astype(BF)

    def plane_reduce(slices, half, bufs, t, small, large, finish):
        piece, row, col = slices
        rb, rp = bufs
        if half == 0:
            bundle = lambda p: row(p, half)
            line = lambda p: piece(y, p, half)
            pos, near, pos2, near2, n1, n2 = y, ydev, x, xdev, NY, NX
        else:
            bundle = lambda p: col(p, half)
            line = lambda p: piece(p, x, half)
            pos, near, pos2, near2, n1, n2 = x, xdev, y, ydev, NX, NY
        for stage, (at, p0, nr, n, rbuf, dt) in enumerate(
            ((bundle, pos, near, n1, rb, large), (line, pos2, near2, n2, rp, small))
        ):
            out = [send(at(wrap(p0 + k, n)), rbuf.at[k - 1], nr(k)) for k in (2, 1, 3)]
            t += dt
            yield t
            for cp in out:
                cp.wait_recv()
            mine = at(p0)
            total = mine[...].astype(F32)
            for k in range(3):
                total = total + rbuf[k].astype(F32)
            if stage == 0:
                mine[...] = total.astype(BF)
            else:
                finish(total)

    def ts_piece(yy, xx, half):
        return tsum.at[pl.ds(4 * half, 4), lax.rem(yy, 2), xx, :, hi(yy)]

    def ts_row(yy, half):
        return tsum.at[pl.ds(4 * half, 4), lax.rem(yy, 2), :, :, hi(yy)]

    def ts_col(xx, half):
        return tsum.at[pl.ds(4 * half, 4), :, xx]

    def g_src(j):
        jl = j - 8 * (1 - c)
        return tfin.at[jl]

    def g_src_fixed(j):
        return tfin.at[0] if isinstance(j, int) else g_src(j)

    def g_dst(j):
        return gvals.at[j, ylow, x, :, hi(y)]

    g_slices = t_slices(gvals)

    def t_half(half):
        yield 20.5
        t_swap[half].wait_recv()
        here = pl.ds(4 * half, 4)
        tsum[here] = (tterm[jset(c, half)].astype(F32) + tr0[here].astype(F32)).astype(BF)

        def finish(total):
            tfin[here] = total.astype(BF)

        yield from plane_reduce(
            (ts_piece, ts_row, ts_col), half, (tr_row if half == 0 else tr_col, tr_piece.at[half]),
            20.5, 3.6, 5.6, finish,
        )

    def t_path():
        yield from until("h", 18.0)
        value_terms()
        yield from both(t_half)
        done = tile_exchange(g_src_fixed, g_dst, lambda j: j)
        yield 37.5
        done()
        yield from both(lambda half: plane_gather(g_slices, half, 37.5, 3.4, 5.5, 1.5))
        gvals_out[...] = gvals[...]

    def ps_piece(yy, xx, half):
        return psum.at[yy, xx, pl.ds(128 * half, 128), :]

    def ps_row(yy, half):
        return psum.at[yy, :, pl.ds(128 * half, 128), :]

    def ps_col(xx, half):
        return psum.at[:, xx, pl.ds(128 * half, 128), :]

    def p_half(half):
        here = pl.ds(128 * half, 128)
        yield from until("g", 24.5 + half)
        yield 25.0 + half
        for q in range(nz):
            pterm[q // NX, q % NX, here, :] = jnp.dot(ggt[here, :], hid[q], preferred_element_type=F32).astype(BF)
        swap = send(
            pterm.at[:, :, here, pl.ds(mult(128 * oc, 128), 128)], pr0.at[half], partner
        )
        yield 28.0 + half
        swap.wait_recv()
        own = pterm[:, :, here, pl.ds(mult(128 * c, 128), 128)]
        psum[:, :, here, :] = (own.astype(F32) + pr0[half].astype(F32)).astype(BF)

        def finish(total):
            gg_out[:, pl.ds(128 * half, 128)] = total.T

        yield from plane_reduce(
            (ps_piece, ps_row, ps_col), half, (pr_bundle.at[half], pr_piece.at[half]), 28.0 + half, 4.3, 8.3, finish
        )

    def aff_path():
        yield from until("g", 25.0)
        yield 26.5
        lane = jnp.bitwise_and(idx[...], 127)
        chunk = lax.shift_right_logical(idx[...], 7)
        acc = jnp.zeros((rows_blk, 128), F32)
        for j in range(nz):
            part = lax.dot_general(mg[...], vals[j].reshape(rows_blk, cols), NT, preferred_element_type=F32)
            got = jnp.take_along_axis(part, lane, axis=1, mode="promise_in_bounds")
            acc = jnp.where(chunk == j, got, acc)
        acc_t = acc.T
        for i in range(nz):
            affp[i] = acc_t[2 * i : 2 * i + 2, :]
        cps = [send(affp.at[wrap(z + k, nz)], affr.at[k], zdev(k)) for k in range(1, nz)]
        yield 35.0
        total = affp[z]
        for k in range(1, nz):
            cps[k - 1].wait_recv()
            total = total + affr[k]
        affall[z] = total
        cps = [send(affall.at[z], affall.at[z], zdev(k)) for k in range(1, nz)]
        yield 43.0
        for cp in cps:
            cp.wait_recv()
        for i in range(nz):
            afft[2 * i : 2 * i + 2, :] = affall[i]
        weights = wgt[...]
        aff = afft[...]
        gs_out[...] = weights * (aff - jnp.sum(weights * aff, axis=0, keepdims=True))

    run_streams(
        [hid_relay(0.0, 4.0), w_path(), v_path(), t_path(), hidden_relay(23.0, 4.0), p_half(0), p_half(1), aff_path()]
    )

    for cp in sent:
        cp.wait_send()


def write_out(nz, bo_in, gh_in, gg_in, gvals_in, gs_in, bo_out, gh_out, gg_out, gv_out, gs_out, wide, sem):
    rows, cols = bo_in.shape
    z = lax.axis_index("table")
    small = ((bo_in, bo_out), (gh_in, gh_out), (gg_in, gg_out), (gs_in, gs_out))
    copies = [pltpu.make_async_copy(src, dst, sem.at[nz + i]) for i, (src, dst) in enumerate(small)]
    for cp in copies:
        cp.start()
    for j in range(nz):
        wide[j] = gvals_in[j].reshape(rows, cols).astype(F32)
        q = wrap(z - j, nz)
        cp = pltpu.make_async_copy(wide.at[j], gv_out.at[:, pl.ds(mult(q * cols, cols), cols)], sem.at[j])
        cp.start()
        copies.append(cp)
    for cp in copies:
        cp.wait()


def layer(nz, hidden_in, gate_weight, values, pick_rows, pick_scores, grad_out):
    rows, cols = hidden_in.shape
    vm = pltpu.VMEM
    scratch = [
        vm((nz, rows, cols), BF),
        vm((NY, NX, 2, rows, cols), BF),
        vm((nz, 2, NX, 16, cols), BF),
        vm((rows, nz * rows), BF),
        vm((nz, rows, rows), BF),
        vm((rows, cols), BF),
        vm((rows, cols), F32),
        vm((rows, cols), BF),
        vm((rows, cols), BF),
        vm((cols, rows), BF),
        vm((rows, 128), F32),
        vm((32, rows), jnp.int32),
        vm((32, rows), jnp.int32),
        vm((32, rows), F32),
        vm((rows, 128), jnp.int32),
        vm((NY, NX, cols, cols), BF),
        vm((2, NY, NX, 128, 128), BF),
        vm((NY, NX, cols, 128), BF),
        vm((2, 3, 4, 128, 128), BF),
        vm((2, 3, 128, 128), BF),
        vm((nz, 2, NX, 16, cols), BF),
        vm((8, 2, NX, 16, cols), BF),
        vm((8, 2, NX, 16, cols), BF),
        vm((3, 4, NX, 16, 128), BF),
        vm((3, 4, 2, 16, cols), BF),
        vm((2, 3, 4, 16, 128), BF),
        vm((8, 16, 128), BF),
        vm((nz, 2, NX, 16, cols), BF),
        vm((nz, rows, cols), BF),
        vm((2, nz // 4, rows, cols), BF),
        vm((2, nz // 4, rows, cols), BF),
        vm((nz, 2, 128), F32),
        vm((nz, 2, 128), F32),
        vm((nz, 2, 128), F32),
        vm((32, 128), F32),
        pltpu.SemaphoreType.DMA((N_COPIES,)),
        pltpu.SemaphoreType.DMA((N_COPIES,)),
        pltpu.SemaphoreType.DMA((N_LOCAL,)),
        pltpu.SemaphoreType.REGULAR((2,)),
    ]
    hbm = pl.BlockSpec(memory_space=pl.ANY)
    vmem = pl.BlockSpec(memory_space=pltpu.VMEM)
    arrays = (hidden_in, gate_weight, values, pick_rows.T, pick_scores.T, grad_out)
    arrays = [pltpu.with_memory_space_constraint(a, pltpu.HBM) for a in arrays]
    parts = pl.pallas_call(
        functools.partial(body, nz),
        out_shape=(
            jax.ShapeDtypeStruct((rows, cols), BF),
            jax.ShapeDtypeStruct((rows, cols), BF),
            jax.ShapeDtypeStruct((rows, cols), F32),
            jax.ShapeDtypeStruct((nz, 2, NX, 16, cols), BF),
            jax.ShapeDtypeStruct((32, rows), F32),
        ),
        in_specs=[pl.BlockSpec(memory_space=pltpu.HBM)] * 6,
        out_specs=(vmem,) * 5,
        scratch_shapes=scratch,
        compiler_params=pltpu.CompilerParams(
            collective_id=0, has_side_effects=True, vmem_limit_bytes=32 * 1024 * 1024
        ),
    )(*arrays)
    bo, gh, gg, gv, gs = pl.pallas_call(
        functools.partial(write_out, nz),
        out_shape=(
            jax.ShapeDtypeStruct((rows, cols), BF),
            jax.ShapeDtypeStruct((rows, cols), BF),
            jax.ShapeDtypeStruct((rows, cols), F32),
            jax.ShapeDtypeStruct((rows, nz * cols), F32),
            jax.ShapeDtypeStruct((32, rows), F32),
        ),
        in_specs=[vmem] * 5,
        out_specs=(hbm,) * 5,
        scratch_shapes=[pltpu.VMEM((nz, rows, cols), F32), pltpu.SemaphoreType.DMA((nz + 4,))],
        compiler_params=pltpu.CompilerParams(vmem_limit_bytes=8 * 1024 * 1024),
    )(*parts)
    return bo, gh, gg, gv, gs.T


def solution(mesh):
    nz = mesh.shape["table"]
    return jax.shard_map(
        functools.partial(layer, nz),
        mesh=mesh,
        in_specs=(
            P("dp", "table"),
            P("dp", "table"),
            P("table", None),
            P("dp", None),
            P("dp", None),
            P("dp", "table"),
        ),
        out_specs=(
            P("dp", "table"),
            P("dp", "table"),
            P("dp", "table"),
            P("table", None),
            P("dp", None),
        ),
        check_vma=False,
    )
```

```python
import functools
import heapq

import jax
import jax.numpy as jnp
from jax import lax
from jax.experimental import pallas as pl
from jax.experimental.pallas import tpu as pltpu
from jax.sharding import PartitionSpec as P

MESH_ID = pl.DeviceIdType.MESH
F32 = jnp.float32
BF = jnp.bfloat16
NX = 4
NY = 4
CHUNKS = 4
N_COPIES = 320
N_LOCAL = 16
NT = (((1,), (1,)), ((), ()))
RELAY = {1: 0, 2: 0, 3: 2, 4: 2, 5: 4, 6: 4, 7: 6, 8: 6}
RING = {k: k - 1 for k in range(1, 9)}


def hop_time(links):
    return 3.4 + 1.0 * (links - 1)


def children_of(parents, node, limit):
    return sorted((k for k, p in parents.items() if p == node and k <= limit), reverse=True)


def wrap(value, size):
    return lax.rem(value + size, size)


def mult(value, unit):
    return pl.multiple_of(value, unit)


def run_streams(streams):
    heap = []
    for order, stream in enumerate(streams):
        heapq.heappush(heap, (0.0, order, stream))
    while heap:
        when, order, stream = heapq.heappop(heap)
        try:
            due = next(stream)
        except StopIteration:
            continue
        heapq.heappush(heap, (due, order, stream))


def body(
    nz,
    hid_in, w_in, val_in, rows_in, score_in, go_in,
    bo_out, gh_out, gg_out, gvals, gs_out,
    hid, wts, vals, spread, spread_t, go, gin, mg, gg, ggt, pad_a, picks, rel_t, wgt, idx,
    pterm, pr0, psum, pr_bundle, pr_piece,
    tterm, tr0, tsum, tr_row, tr_col, tr_piece, tfin,
    iterm, ri, affp, affr, affall, afft,
    send_sem, recv_sem, local_sem, know,
):
    rows_blk = hid_in.shape[0]
    cols = hid_in.shape[1]
    b = lax.axis_index("dp")
    z = lax.axis_index("table")
    c = lax.rem(b, 2)
    x = lax.rem(lax.div(b, 2), NX)
    y = lax.div(b, 2 * NX)
    s = 1 - 2 * c
    oc = 1 - c

    def dev(yy, xx, cc):
        return ((yy * NX + xx) * 2 + cc, z)

    def zdev(delta):
        return (b, wrap(z + delta, nz))

    def xdev(delta):
        return dev(y, wrap(x + delta, NX), c)

    def ydev(delta):
        return dev(wrap(y + delta, NY), x, c)

    partner = dev(y, x, oc)

    barrier = pltpu.get_barrier_semaphore()
    peers = [zdev(k) for k in (1, -1, 2, -2)] + [xdev(k) for k in (1, 2, 3)] + [ydev(k) for k in (1, 2, 3)]
    peers.append(partner)
    for peer in peers:
        pl.semaphore_signal(barrier, inc=1, device_id=peer, device_id_type=MESH_ID)

    local_count = [0]
    copy_count = [0]
    sent = []

    def lcopy(src, dst):
        i = local_count[0]
        local_count[0] += 1
        cp = pltpu.make_async_copy(src, dst, local_sem.at[i])
        cp.start()
        return cp

    def send(src, dst, peer):
        i = copy_count[0]
        copy_count[0] += 1
        cp = pltpu.make_async_remote_copy(
            src_ref=src, dst_ref=dst, send_sem=send_sem.at[i], recv_sem=recv_sem.at[i],
            device_id=peer, device_id_type=MESH_ID,
        )
        cp.start()
        sent.append(cp)
        return cp

    own_rows = lcopy(rows_in, picks)
    own_scores = lcopy(score_in, wgt)
    own_w = lcopy(w_in, wts.at[y, x, c])
    own_h = lcopy(hid_in, hid.at[z])
    own_g = lcopy(go_in, go)

    ylow = lax.rem(y, 2)
    yhigh = lax.div(y, 2)

    pad_a[...] = jnp.zeros_like(pad_a)
    own_rows.wait()
    own_scores.wait()
    pad_a[0:32, :] = picks[...].astype(F32)
    total_rows = nz * rows_blk

    def relative(row_f):
        shifted = row_f.astype(jnp.int32) + (total_rows - rows_blk * z)
        return jnp.where(shifted >= total_rows, shifted - total_rows, shifted)

    idx[...] = relative(pad_a[...].T)
    rel_t[...] = relative(pad_a[0:32, :])
    scores = wgt[...]
    expo = jnp.exp(scores - jnp.max(scores, axis=0, keepdims=True))
    wgt[...] = expo / jnp.sum(expo, axis=0, keepdims=True)
    weights_bf = wgt[...].astype(BF).astype(F32)
    afft[...] = weights_bf

    def spread_block(i, carry):
        ids = lax.broadcasted_iota(jnp.int32, (rows_blk, rows_blk), 0) + i * rows_blk
        acc = jnp.zeros((rows_blk, rows_blk), F32)
        for k in range(32):
            acc = jnp.where(rel_t[k : k + 1, :] == ids, afft[k : k + 1, :], acc)
        spread_t[i] = acc.astype(BF)
        spread[:, pl.ds(mult(i * rows_blk, rows_blk), rows_blk)] = acc.T.astype(BF)
        return carry

    own_w.wait()
    own_h.wait()
    own_g.wait()
    pl.semaphore_wait(barrier, len(peers))

    def w_piece(yy, xx, cc, half):
        return wts.at[yy, xx, cc, :, pl.ds(128 * half, 128)]

    def w_row(yy, cc, half):
        return wts.at[yy, :, cc, :, pl.ds(128 * half, 128)]

    def w_col(xx, cc, half):
        return wts.at[:, xx, cc, :, pl.ds(128 * half, 128)]

    def jset(cc, half):
        return pl.ds(8 * (1 - cc) + 4 * half, 4)

    def hi(yy):
        return pl.ds(mult(128 * lax.div(yy, 2), 128), 128)

    def t_slices(buf):
        def piece(yy, xx, cc, half):
            return buf.at[jset(cc, half), lax.rem(yy, 2), xx, :, hi(yy)]

        def row(yy, cc, half):
            return buf.at[jset(cc, half), lax.rem(yy, 2), :, :, hi(yy)]

        def col(xx, cc, half):
            return buf.at[jset(cc, half), :, xx]

        return piece, row, col

    flags = set()

    def until(name, t):
        while name not in flags:
            yield t
            t += 0.5

    def both(make):
        live = [make(half) for half in (0, 1)]
        while live:
            due = None
            for part in list(live):
                try:
                    due = next(part)
                except StopIteration:
                    live.remove(part)
            if live:
                yield due

    def plane_gather(slices, half, t, first_step, second_step, third_step):
        piece, row, col = slices
        if half == 0:
            line = lambda p: piece(y, p, c, half)
            bundle = lambda p: row(p, c, half)
            pos, near, pos2, near2, n1, n2 = x, xdev, y, ydev, NX, NY
        else:
            line = lambda p: piece(p, x, c, half)
            bundle = lambda p: col(p, c, half)
            pos, near, pos2, near2, n1, n2 = y, ydev, x, xdev, NY, NX
        out = [send(line(pos), line(pos), near(k)) for k in (2, 1, 3)]
        t += first_step
        yield t
        for cp in out:
            cp.wait_recv()
        out = [send(bundle(pos2), bundle(pos2), near2(k)) for k in (2, 1, 3)]
        swap = [send(bundle(pos2), bundle(pos2), partner)]
        t += second_step
        yield t
        for k, cp in ((1, out[1]), (3, out[2]), (2, out[0])):
            cp.wait_recv()
            p = wrap(pos2 - k, n2)
            swap.append(send(bundle(p), bundle(p), partner))
        t += third_step
        yield t
        for cp in swap:
            cp.wait_recv()

    pending = []
    first = [True]

    def accumulate(block):
        q = wrap(z + block, nz)
        part = jnp.dot(
            hid[q], wts[lax.div(q, NX), lax.rem(q, NX)].reshape(cols, cols), preferred_element_type=F32
        )
        if first[0]:
            gin[...] = part
            first[0] = False
        else:
            gin[...] += part

    arrived = {}

    def block_here(block, parts):
        arrived[block] = arrived.get(block, 0) + parts
        if arrived[block] == CHUNKS:
            if "w" in flags:
                accumulate(block)
            else:
                pending.append(block)

    span = rows_blk // CHUNKS

    def hid_chunk(block, ch):
        return hid.at[wrap(z + block, nz), pl.ds(span * ch, span), :]

    def limits(ch):
        up = nz // 2 if ch % 2 == 0 else nz // 2 - 1
        return ((1, up), (-1, nz - 1 - up))

    def hid_relay(t):
        waiting = []

        def pass_on(ch, sign, limit, k, now):
            at = hid_chunk(-sign * k, ch)
            for child in children_of(RELAY, k, limit):
                cp = send(at, at, zdev(sign * (child - k)))
                leaf = 0.0 if children_of(RELAY, child, limit) else 2.0
                heapq.heappush(waiting, (now + hop_time(child - k) + leaf, len(sent), ch, sign, limit, child, cp))

        for ch in range(CHUNKS):
            for sign, limit in limits(ch):
                pass_on(ch, sign, limit, 0, t + 0.3 * ch)
        block_here(0, CHUNKS)
        while waiting:
            yield waiting[0][0]
            now, _, ch, sign, limit, k, cp = heapq.heappop(waiting)
            cp.wait_recv()
            pass_on(ch, sign, limit, k, now)
            block_here((-sign * k) % nz, 1)
        yield from until("w", now)
        flags.add("h")

    def tile_exchange(make_src, make_dst, toward):
        cps = []
        for i in range(1, nz // 2):
            j = jnp.where(c == 0, nz - i, i)
            cps.append(send(make_src(j), make_dst(j), (b, wrap(z + toward(j), nz))))
        half = nz // 2
        i = copy_count[0]
        copy_count[0] += 1
        last = pltpu.make_async_remote_copy(
            src_ref=make_src(half), dst_ref=make_dst(half), send_sem=send_sem.at[i], recv_sem=recv_sem.at[i],
            device_id=zdev(half), device_id_type=MESH_ID,
        )
        i = local_count[0]
        local_count[0] += 1
        own = pltpu.make_async_copy(make_src(0), make_dst(0), local_sem.at[i])

        @pl.when(c == 0)
        def _():
            last.start()

        @pl.when(c == 1)
        def _():
            own.start()

        def finish():
            for cp in cps:
                cp.wait_recv()

            @pl.when(c == 0)
            def _():
                last.wait()

            @pl.when(c == 1)
            def _():
                own.wait()

        return finish

    v_slices = t_slices(vals)
    tile_rows = lax.rem(y, 2) * NX + x

    def val_src(j):
        zd = wrap(z - j, nz)
        return val_in.at[pl.ds(mult(16 * tile_rows, 16), 16), pl.ds(mult(cols * zd + 128 * yhigh, 128), 128)]

    def val_dst(j):
        return vals.at[j, ylow, x, :, hi(y)]

    def both(make):
        parts = [make(half) for half in (0, 1)]
        live = list(parts)
        while live:
            due = None
            for part in list(live):
                try:
                    due = next(part)
                except StopIteration:
                    live.remove(part)
            if live:
                yield due

    def v_path():
        for stage, reach in enumerate((2, 4)):
            for sign in (1, -1):
                pl.semaphore_signal(know.at[stage], inc=1, device_id=zdev(sign * reach), device_id_type=MESH_ID)
            yield (1.5, 4.0)[stage]
            pl.semaphore_wait(know.at[stage], 2)
        finish = tile_exchange(val_src, val_dst, lambda j: nz - j)
        yield 13.5
        finish()
        yield from both(lambda half: plane_gather(v_slices, half, 13.5, 3.5, 6.0, 2.0))
        flags.add("v")

    w_slices = (w_piece, w_row, w_col)

    def spread_path():
        yield 0.2
        lax.fori_loop(0, nz, spread_block, 0)

    def w_path():
        yield from both(lambda half: plane_gather(w_slices, half, 0.0, 3.5, 9.0, 2.0))
        flags.add("w")
        for block in pending:
            accumulate(block)
        pending.clear()

    def gate_parts():
        gate = gin[...]
        sig = jax.nn.sigmoid(gate)
        return gate, sig, go[...].astype(F32)

    t_swap = []

    def value_terms():
        gate, sig, upstream = gate_parts()
        mg[...] = (upstream * (gate * sig)).astype(BF)
        for owner in (oc, c):
            for jl in range(8):
                j = 8 * (1 - owner) + jl
                tterm[j] = (
                    jnp.dot(spread_t[j], mg[...], preferred_element_type=F32).astype(BF).reshape(2, NX, 16, cols)
                )
            if not t_swap:
                t_swap.extend(send(tterm.at[jset(oc, h)], tr0.at[pl.ds(4 * h, 4)], partner) for h in (0, 1))

    def gate_gradient():
        gate, sig, upstream = gate_parts()
        memory_read = jnp.dot(spread[...], vals[...].reshape(total_rows, cols), preferred_element_type=F32)
        bo_out[...] = (memory_read * (gate * sig)).astype(BF)
        slope = (upstream * memory_read * (sig * (1.0 + gate * (1.0 - sig)))).astype(BF)
        gg[...] = slope
        ggt[...] = slope.astype(F32).T.astype(BF)

    def make_iterm(block):
        q = wrap(z + block, nz)
        iterm[q] = lax.dot_general(
            gg[...], wts[lax.div(q, NX), lax.rem(q, NX)].reshape(cols, cols), NT, preferred_element_type=F32
        ).astype(BF)

    made = set()

    def need_iterm(block):
        if block % nz not in made:
            made.add(block % nz)
            make_iterm(block)

    def i_chunk(block, ch):
        return iterm.at[wrap(z + block, nz), pl.ds(span * ch, span), :]

    def hidden_relay(t):
        yield from until("v", t)
        gate_gradient()
        flags.add("g")
        ready = []
        flying = {}

        def mature(ch, sign, limit, k):
            kids = children_of(RING, k, limit)
            return max((mature(ch, sign, limit, kid) + hop_time(kid - k) for kid in kids), default=0.3 * ch)

        def depth(ch, k):
            return 0 if k == 0 else depth(ch, RING[k]) + 1

        for ch in range(CHUNKS):
            for sign, limit in limits(ch):
                for k in range(limit + 1):
                    ready.append((mature(ch, sign, limit, k), -depth(ch, k), len(ready), ch, sign, limit, k))
        ends = {}
        start = t + 0.5
        for when, _, _, ch, sign, limit, k in sorted(ready):
            yield start + when
            need_iterm(sign * k)
            here = pl.ds(span * ch, span)
            side = (1 - sign) // 2
            q = wrap(z + sign * k, nz)
            kids = children_of(RING, k, limit)
            if kids:
                total = iterm[q, here, :].astype(F32) if k or ch not in ends else gin[here, :]
                for kid in kids:
                    flying[ch, sign, kid].wait_recv()
                    total = total + ri[side, kid - 1, here, :].astype(F32)
                if k:
                    iterm[q, here, :] = total.astype(BF)
                elif ch in ends:
                    gh_out[here, :] = total.astype(BF)
                else:
                    gin[here, :] = total
                    ends[ch] = True
            if k:
                parent = RING[k]
                flying[ch, sign, k] = send(i_chunk(sign * k, ch), ri.at[side, k - 1, here, :], zdev(sign * (k - parent)))

    def plane_reduce(slices, half, bufs, t, small, large, finish):
        piece, row, col = slices
        rb, rp = bufs
        if half == 0:
            bundle = lambda p: row(p, half)
            line = lambda p: piece(y, p, half)
            pos, near, pos2, near2, n1, n2 = y, ydev, x, xdev, NY, NX
        else:
            bundle = lambda p: col(p, half)
            line = lambda p: piece(p, x, half)
            pos, near, pos2, near2, n1, n2 = x, xdev, y, ydev, NX, NY
        for stage, (at, p0, nr, n, rbuf, dt) in enumerate(
            ((bundle, pos, near, n1, rb, large), (line, pos2, near2, n2, rp, small))
        ):
            out = [send(at(wrap(p0 + k, n)), rbuf.at[k - 1], nr(k)) for k in (2, 1, 3)]
            t += dt
            yield t
            for cp in out:
                cp.wait_recv()
            mine = at(p0)
            total = mine[...].astype(F32)
            for k in range(3):
                total = total + rbuf[k].astype(F32)
            if stage == 0:
                mine[...] = total.astype(BF)
            else:
                finish(total)

    def ts_piece(yy, xx, half):
        return tsum.at[pl.ds(4 * half, 4), lax.rem(yy, 2), xx, :, hi(yy)]

    def ts_row(yy, half):
        return tsum.at[pl.ds(4 * half, 4), lax.rem(yy, 2), :, :, hi(yy)]

    def ts_col(xx, half):
        return tsum.at[pl.ds(4 * half, 4), :, xx]

    def g_src(j):
        jl = j - 8 * (1 - c)
        return tfin.at[jl]

    def g_src_fixed(j):
        return tfin.at[0] if isinstance(j, int) else g_src(j)

    def g_dst(j):
        return gvals.at[j, ylow, x, :, hi(y)]

    g_slices = t_slices(gvals)

    def t_half(half):
        yield 22.0
        t_swap[half].wait_recv()
        here = pl.ds(4 * half, 4)
        tsum[here] = (tterm[jset(c, half)].astype(F32) + tr0[here].astype(F32)).astype(BF)

        def finish(total):
            tfin[here] = total.astype(BF)

        yield from plane_reduce(
            (ts_piece, ts_row, ts_col), half, (tr_row if half == 0 else tr_col, tr_piece.at[half]),
            22.0, 4.0, 6.0, finish,
        )

    def t_path():
        yield from until("h", 18.5)
        value_terms()
        yield from both(t_half)
        done = tile_exchange(g_src_fixed, g_dst, lambda j: j)
        yield 40.0
        done()
        yield from both(lambda half: plane_gather(g_slices, half, 40.0, 3.5, 5.5, 2.0))

    def ps_piece(yy, xx, half):
        return psum.at[yy, xx, pl.ds(128 * half, 128), :]

    def ps_row(yy, half):
        return psum.at[yy, :, pl.ds(128 * half, 128), :]

    def ps_col(xx, half):
        return psum.at[:, xx, pl.ds(128 * half, 128), :]

    def p_half(half):
        here = pl.ds(128 * half, 128)
        yield from until("g", 25.5 + half)
        yield 28.2 + half
        for q in range(nz):
            pterm[q // NX, q % NX, here, :] = jnp.dot(ggt[here, :], hid[q], preferred_element_type=F32).astype(BF)
        swap = send(
            pterm.at[:, :, here, pl.ds(mult(128 * oc, 128), 128)], pr0.at[half], partner
        )
        yield 32.0 + half
        swap.wait_recv()
        own = pterm[:, :, here, pl.ds(mult(128 * c, 128), 128)]
        psum[:, :, here, :] = (own.astype(F32) + pr0[half].astype(F32)).astype(BF)

        def finish(total):
            gg_out[:, pl.ds(128 * half, 128)] = total.T

        yield from plane_reduce(
            (ps_piece, ps_row, ps_col), half, (pr_bundle.at[half], pr_piece.at[half]), 32.0 + half, 4.5, 8.5, finish
        )

    def aff_path():
        yield from until("g", 26.0)
        yield 30.0
        lane = jnp.bitwise_and(idx[...], 127)
        chunk = lax.shift_right_logical(idx[...], 7)
        acc = jnp.zeros((rows_blk, 128), F32)
        for j in range(nz):
            part = lax.dot_general(mg[...], vals[j].reshape(rows_blk, cols), NT, preferred_element_type=F32)
            got = jnp.take_along_axis(part, lane, axis=1, mode="promise_in_bounds")
            acc = jnp.where(chunk == j, got, acc)
        acc_t = acc.T
        for i in range(nz):
            affp[i] = acc_t[2 * i : 2 * i + 2, :]
        cps = [send(affp.at[wrap(z + k, nz)], affr.at[k], zdev(k)) for k in range(1, nz)]
        yield 38.5
        total = affp[z]
        for k in range(1, nz):
            cps[k - 1].wait_recv()
            total = total + affr[k]
        affall[z] = total
        cps = [send(affall.at[z], affall.at[z], zdev(k)) for k in range(1, nz)]
        yield 46.5
        for cp in cps:
            cp.wait_recv()
        for i in range(nz):
            afft[2 * i : 2 * i + 2, :] = affall[i]
        weights = wgt[...]
        aff = afft[...]
        gs_out[...] = weights * (aff - jnp.sum(weights * aff, axis=0, keepdims=True))

    run_streams(
        [v_path(), hid_relay(0.0), w_path(), spread_path(), t_path(), hidden_relay(25.2), p_half(0), p_half(1), aff_path()]
    )

    for cp in sent:
        cp.wait_send()


def write_out(nz, bo_in, gh_in, gg_in, gvals_in, gs_in, bo_out, gh_out, gg_out, gv_out, gs_out, wide, sem):
    rows, cols = bo_in.shape
    z = lax.axis_index("table")
    small = ((bo_in, bo_out), (gh_in, gh_out), (gg_in, gg_out), (gs_in, gs_out))
    copies = [pltpu.make_async_copy(src, dst, sem.at[nz + i]) for i, (src, dst) in enumerate(small)]
    for cp in copies:
        cp.start()
    for j in range(nz):
        wide[j] = gvals_in[j].reshape(rows, cols).astype(F32)
        q = wrap(z - j, nz)
        cp = pltpu.make_async_copy(wide.at[j], gv_out.at[:, pl.ds(mult(q * cols, cols), cols)], sem.at[j])
        cp.start()
        copies.append(cp)
    for cp in copies:
        cp.wait()


def layer(nz, hidden_in, gate_weight, values, pick_rows, pick_scores, grad_out):
    rows, cols = hidden_in.shape
    vm = pltpu.VMEM
    scratch = [
        vm((nz, rows, cols), BF),
        vm((NY, NX, 2, rows, cols), BF),
        vm((nz, 2, NX, 16, cols), BF),
        vm((rows, nz * rows), BF),
        vm((nz, rows, rows), BF),
        vm((rows, cols), BF),
        vm((rows, cols), F32),
        vm((rows, cols), BF),
        vm((rows, cols), BF),
        vm((cols, rows), BF),
        vm((rows, 128), F32),
        vm((32, rows), jnp.int32),
        vm((32, rows), jnp.int32),
        vm((32, rows), F32),
        vm((rows, 128), jnp.int32),
        vm((NY, NX, cols, cols), BF),
        vm((2, NY, NX, 128, 128), BF),
        vm((NY, NX, cols, 128), BF),
        vm((2, 3, 4, 128, 128), BF),
        vm((2, 3, 128, 128), BF),
        vm((nz, 2, NX, 16, cols), BF),
        vm((8, 2, NX, 16, cols), BF),
        vm((8, 2, NX, 16, cols), BF),
        vm((3, 4, NX, 16, 128), BF),
        vm((3, 4, 2, 16, cols), BF),
        vm((2, 3, 4, 16, 128), BF),
        vm((8, 16, 128), BF),
        vm((nz, rows, cols), BF),
        vm((2, nz // 2, rows, cols), BF),
        vm((nz, 2, 128), F32),
        vm((nz, 2, 128), F32),
        vm((nz, 2, 128), F32),
        vm((32, 128), F32),
        pltpu.SemaphoreType.DMA((N_COPIES,)),
        pltpu.SemaphoreType.DMA((N_COPIES,)),
        pltpu.SemaphoreType.DMA((N_LOCAL,)),
        pltpu.SemaphoreType.REGULAR((2,)),
    ]
    hbm = pl.BlockSpec(memory_space=pl.ANY)
    vmem = pl.BlockSpec(memory_space=pltpu.VMEM)
    arrays = (hidden_in, gate_weight, values, pick_rows.T, pick_scores.T, grad_out)
    arrays = [pltpu.with_memory_space_constraint(a, pltpu.HBM) for a in arrays]
    parts = pl.pallas_call(
        functools.partial(body, nz),
        out_shape=(
            jax.ShapeDtypeStruct((rows, cols), BF),
            jax.ShapeDtypeStruct((rows, cols), BF),
            jax.ShapeDtypeStruct((rows, cols), F32),
            jax.ShapeDtypeStruct((nz, 2, NX, 16, cols), BF),
            jax.ShapeDtypeStruct((32, rows), F32),
        ),
        in_specs=[pl.BlockSpec(memory_space=pltpu.HBM)] * 6,
        out_specs=(vmem, vmem, vmem, hbm, vmem),
        scratch_shapes=scratch,
        compiler_params=pltpu.CompilerParams(
            collective_id=0, has_side_effects=True, vmem_limit_bytes=32 * 1024 * 1024
        ),
    )(*arrays)
    bo, gh, gg, gv, gs = pl.pallas_call(
        functools.partial(write_out, nz),
        out_shape=(
            jax.ShapeDtypeStruct((rows, cols), BF),
            jax.ShapeDtypeStruct((rows, cols), BF),
            jax.ShapeDtypeStruct((rows, cols), F32),
            jax.ShapeDtypeStruct((rows, nz * cols), F32),
            jax.ShapeDtypeStruct((32, rows), F32),
        ),
        in_specs=[vmem] * 5,
        out_specs=(hbm,) * 5,
        scratch_shapes=[pltpu.VMEM((nz, rows, cols), F32), pltpu.SemaphoreType.DMA((nz + 4,))],
        compiler_params=pltpu.CompilerParams(vmem_limit_bytes=8 * 1024 * 1024),
    )(*parts)
    return bo, gh, gg, gv, gs.T


def solution(mesh):
    nz = mesh.shape["table"]
    return jax.shard_map(
        functools.partial(layer, nz),
        mesh=mesh,
        in_specs=(
            P("dp", "table"),
            P("dp", "table"),
            P("table", None),
            P("dp", None),
            P("dp", None),
            P("dp", "table"),
        ),
        out_specs=(
            P("dp", "table"),
            P("dp", "table"),
            P("dp", "table"),
            P("table", None),
            P("dp", None),
        ),
        check_vma=False,
    )
```

```python
import functools
import heapq

import jax
import jax.numpy as jnp
from jax import lax
from jax.experimental import pallas as pl
from jax.experimental.pallas import tpu as pltpu
from jax.sharding import PartitionSpec as P

MESH_ID = pl.DeviceIdType.MESH
F32 = jnp.float32
BF = jnp.bfloat16
NX = 4
NY = 4
CHUNKS = 4
N_COPIES = 320
N_LOCAL = 16
T0 = 22.0
NT = (((1,), (1,)), ((), ()))
RELAY = {1: 0, 2: 0, 3: 2, 4: 2, 5: 4, 6: 4, 7: 6, 8: 6}
RING = {k: k - 1 for k in range(1, 9)}


def hop_time(links):
    return 3.4 + 1.0 * (links - 1)


def children_of(parents, node, limit):
    return sorted((k for k, p in parents.items() if p == node and k <= limit), reverse=True)


def wrap(value, size):
    return lax.rem(value + size, size)


def mult(value, unit):
    return pl.multiple_of(value, unit)


def run_streams(streams):
    heap = []
    for order, stream in enumerate(streams):
        heapq.heappush(heap, (0.0, order, stream))
    while heap:
        when, order, stream = heapq.heappop(heap)
        try:
            due = next(stream)
        except StopIteration:
            continue
        heapq.heappush(heap, (due, order, stream))


def body(
    nz,
    hid_in, w_in, val_in, rows_in, score_in, go_in,
    bo_out, gh_out, gg_out, gvals, gs_out,
    hid, wts, vals, spread, spread_t, go, gin, mg, gg, ggt, pad_a, picks, rel_t, wgt, idx,
    pterm, pr0, psum, pr_bundle, pr_piece,
    pair_t, pair_mg, tsum, tr_row, tr_col, tr_piece, tfin,
    iterm, ri, affp, affr, affall, afft,
    send_sem, recv_sem, local_sem, know,
):
    rows_blk = hid_in.shape[0]
    cols = hid_in.shape[1]
    b = lax.axis_index("dp")
    z = lax.axis_index("table")
    c = lax.rem(b, 2)
    x = lax.rem(lax.div(b, 2), NX)
    y = lax.div(b, 2 * NX)
    s = 1 - 2 * c
    oc = 1 - c

    def dev(yy, xx, cc):
        return ((yy * NX + xx) * 2 + cc, z)

    def zdev(delta):
        return (b, wrap(z + delta, nz))

    def xdev(delta):
        return dev(y, wrap(x + delta, NX), c)

    def ydev(delta):
        return dev(wrap(y + delta, NY), x, c)

    partner = dev(y, x, oc)

    barrier = pltpu.get_barrier_semaphore()
    peers = [zdev(k) for k in (1, -1, 2, -2)] + [xdev(k) for k in (1, 2, 3)] + [ydev(k) for k in (1, 2, 3)]
    peers.append(partner)
    for peer in peers:
        pl.semaphore_signal(barrier, inc=1, device_id=peer, device_id_type=MESH_ID)

    local_count = [0]
    copy_count = [0]
    sent = []

    def lcopy(src, dst):
        i = local_count[0]
        local_count[0] += 1
        cp = pltpu.make_async_copy(src, dst, local_sem.at[i])
        cp.start()
        return cp

    def send(src, dst, peer):
        i = copy_count[0]
        copy_count[0] += 1
        cp = pltpu.make_async_remote_copy(
            src_ref=src, dst_ref=dst, send_sem=send_sem.at[i], recv_sem=recv_sem.at[i],
            device_id=peer, device_id_type=MESH_ID,
        )
        cp.start()
        sent.append(cp)
        return cp

    own_h = lcopy(hid_in, hid.at[z])
    own_w = lcopy(w_in, wts.at[y, x, c])
    own_rows = lcopy(rows_in, picks)
    own_scores = lcopy(score_in, wgt)
    own_g = lcopy(go_in, go)

    ylow = lax.rem(y, 2)
    yhigh = lax.div(y, 2)

    total_rows = nz * rows_blk

    def relative(row_f):
        shifted = row_f.astype(jnp.int32) + (total_rows - rows_blk * z)
        return jnp.where(shifted >= total_rows, shifted - total_rows, shifted)

    def spread_block(i, carry):
        ids = lax.broadcasted_iota(jnp.int32, (rows_blk, rows_blk), 0) + i * rows_blk
        acc = jnp.zeros((rows_blk, rows_blk), F32)
        for k in range(32):
            acc = jnp.where(rel_t[k : k + 1, :] == ids, afft[k : k + 1, :], acc)
        spread_t[i] = acc.astype(BF)
        spread[:, pl.ds(mult(i * rows_blk, rows_blk), rows_blk)] = acc.T.astype(BF)
        return carry

    own_h.wait()
    pl.semaphore_wait(barrier, len(peers))

    def w_piece(yy, xx, cc, half):
        return wts.at[yy, xx, cc, :, pl.ds(128 * half, 128)]

    def w_row(yy, cc, half):
        return wts.at[yy, :, cc, :, pl.ds(128 * half, 128)]

    def w_col(xx, cc, half):
        return wts.at[:, xx, cc, :, pl.ds(128 * half, 128)]

    def jset(cc, half):
        return pl.ds(8 * (1 - cc) + 4 * half, 4)

    def hi(yy):
        return pl.ds(mult(128 * lax.div(yy, 2), 128), 128)

    def t_slices(buf):
        def piece(yy, xx, cc, half):
            return buf.at[jset(cc, half), lax.rem(yy, 2), xx, :, hi(yy)]

        def row(yy, cc, half):
            return buf.at[jset(cc, half), lax.rem(yy, 2), :, :, hi(yy)]

        def col(xx, cc, half):
            return buf.at[jset(cc, half), :, xx]

        return piece, row, col

    flags = set()

    def until(name, t):
        while name not in flags:
            yield t
            t += 0.5

    def both(make):
        live = [make(half) for half in (0, 1)]
        while live:
            due = None
            for part in list(live):
                try:
                    due = next(part)
                except StopIteration:
                    live.remove(part)
            if live:
                yield due

    def plane_gather(slices, half, t, first_step, second_step, third_step):
        piece, row, col = slices
        if half == 0:
            line = lambda p: piece(y, p, c, half)
            bundle = lambda p: row(p, c, half)
            pos, near, pos2, near2, n1, n2 = x, xdev, y, ydev, NX, NY
        else:
            line = lambda p: piece(p, x, c, half)
            bundle = lambda p: col(p, c, half)
            pos, near, pos2, near2, n1, n2 = y, ydev, x, xdev, NY, NX
        out = [send(line(pos), line(pos), near(k)) for k in (2, 1, 3)]
        t += first_step
        yield t
        for cp in out:
            cp.wait_recv()
        out = [send(bundle(pos2), bundle(pos2), near2(k)) for k in (2, 1, 3)]
        swap = [send(bundle(pos2), bundle(pos2), partner)]
        t += second_step
        yield t
        for k, cp in ((1, out[1]), (3, out[2]), (2, out[0])):
            cp.wait_recv()
            p = wrap(pos2 - k, n2)
            swap.append(send(bundle(p), bundle(p), partner))
        t += third_step
        yield t
        for cp in swap:
            cp.wait_recv()

    pending = []
    first = [True]

    def accumulate(block):
        q = wrap(z + block, nz)
        part = jnp.dot(
            hid[q], wts[lax.div(q, NX), lax.rem(q, NX)].reshape(cols, cols), preferred_element_type=F32
        )
        if first[0]:
            gin[...] = part
            first[0] = False
        else:
            gin[...] += part

    arrived = {}

    def block_here(block, parts):
        arrived[block] = arrived.get(block, 0) + parts
        if arrived[block] == CHUNKS:
            if "w" in flags:
                accumulate(block)
            else:
                pending.append(block)

    span = rows_blk // CHUNKS

    def hid_chunk(block, ch):
        return hid.at[wrap(z + block, nz), pl.ds(span * ch, span), :]

    def limits(ch):
        up = nz // 2 if ch % 2 == 0 else nz // 2 - 1
        return ((1, up), (-1, nz - 1 - up))

    def hid_relay(t):
        waiting = []

        def pass_on(ch, sign, limit, k, now):
            at = hid_chunk(-sign * k, ch)
            for child in children_of(RELAY, k, limit):
                cp = send(at, at, zdev(sign * (child - k)))
                leaf = 0.0 if children_of(RELAY, child, limit) else 2.0
                heapq.heappush(waiting, (now + hop_time(child - k) + leaf, len(sent), ch, sign, limit, child, cp))

        for ch in range(CHUNKS):
            for sign, limit in limits(ch):
                pass_on(ch, sign, limit, 0, t + 0.3 * ch)
        block_here(0, CHUNKS)
        while waiting:
            yield waiting[0][0]
            now, _, ch, sign, limit, k, cp = heapq.heappop(waiting)
            cp.wait_recv()
            pass_on(ch, sign, limit, k, now)
            block_here((-sign * k) % nz, 1)
        yield from until("w", now)
        flags.add("h")

    def tile_exchange(make_src, make_dst, toward):
        cps = []
        for i in range(1, nz // 2):
            j = jnp.where(c == 0, nz - i, i)
            cps.append(send(make_src(j), make_dst(j), (b, wrap(z + toward(j), nz))))
        half = nz // 2
        i = copy_count[0]
        copy_count[0] += 1
        last = pltpu.make_async_remote_copy(
            src_ref=make_src(half), dst_ref=make_dst(half), send_sem=send_sem.at[i], recv_sem=recv_sem.at[i],
            device_id=zdev(half), device_id_type=MESH_ID,
        )
        i = local_count[0]
        local_count[0] += 1
        own = pltpu.make_async_copy(make_src(0), make_dst(0), local_sem.at[i])

        @pl.when(c == 0)
        def _():
            last.start()

        @pl.when(c == 1)
        def _():
            own.start()

        def finish():
            for cp in cps:
                cp.wait_recv()

            @pl.when(c == 0)
            def _():
                last.wait()

            @pl.when(c == 1)
            def _():
                own.wait()

        return finish

    v_slices = t_slices(vals)
    tile_rows = lax.rem(y, 2) * NX + x

    def val_src(j):
        zd = wrap(z - j, nz)
        return val_in.at[pl.ds(mult(16 * tile_rows, 16), 16), pl.ds(mult(cols * zd + 128 * yhigh, 128), 128)]

    def val_dst(j):
        return vals.at[j, ylow, x, :, hi(y)]

    def both(make):
        parts = [make(half) for half in (0, 1)]
        live = list(parts)
        while live:
            due = None
            for part in list(live):
                try:
                    due = next(part)
                except StopIteration:
                    live.remove(part)
            if live:
                yield due

    def v_path():
        for stage, reach in enumerate((2, 4)):
            for sign in (1, -1):
                pl.semaphore_signal(know.at[stage], inc=1, device_id=zdev(sign * reach), device_id_type=MESH_ID)
            yield (1.5, 4.0)[stage]
            pl.semaphore_wait(know.at[stage], 2)
        finish = tile_exchange(val_src, val_dst, lambda j: nz - j)
        yield 13.5
        finish()
        yield from both(lambda half: plane_gather(v_slices, half, 13.5, 3.5, 6.0, 2.0))
        flags.add("v")

    w_slices = (w_piece, w_row, w_col)

    def spread_path():
        yield 0.2
        pad_a[...] = jnp.zeros_like(pad_a)
        own_rows.wait()
        own_scores.wait()
        pad_a[0:32, :] = picks[...].astype(F32)
        idx[...] = relative(pad_a[...].T)
        rel_t[...] = relative(pad_a[0:32, :])
        scores = wgt[...]
        expo = jnp.exp(scores - jnp.max(scores, axis=0, keepdims=True))
        wgt[...] = expo / jnp.sum(expo, axis=0, keepdims=True)
        afft[...] = wgt[...].astype(BF).astype(F32)
        lax.fori_loop(0, nz, spread_block, 0)
        own_g.wait()
        pair_t[:, :, 0:128] = spread_t[pl.ds(8 * (1 - c), 8)]
        share = send(spread_t.at[pl.ds(8 * (1 - oc), 8)], pair_t.at[:, :, pl.ds(128, 128)], partner)
        yield 8.0
        share.wait_recv()

    def w_path():
        own_w.wait()
        yield from both(lambda half: plane_gather(w_slices, half, 0.0, 3.5, 9.0, 2.0))
        flags.add("w")
        for block in pending:
            accumulate(block)
        pending.clear()

    def gate_parts():
        gate = gin[...]
        sig = jax.nn.sigmoid(gate)
        return gate, sig, go[...].astype(F32)

    t_swap = []

    def value_terms():
        gate, sig, upstream = gate_parts()
        mg[...] = (upstream * (gate * sig)).astype(BF)
        pair_mg[0:128, :] = mg[...]
        t_swap.append(send(mg, pair_mg.at[pl.ds(128, 128)], partner))

    def gate_gradient():
        gate, sig, upstream = gate_parts()
        memory_read = jnp.dot(spread[...], vals[...].reshape(total_rows, cols), preferred_element_type=F32)
        bo_out[...] = (memory_read * (gate * sig)).astype(BF)
        slope = (upstream * memory_read * (sig * (1.0 + gate * (1.0 - sig)))).astype(BF)
        gg[...] = slope
        ggt[...] = slope.astype(F32).T.astype(BF)

    def make_iterm(block):
        q = wrap(z + block, nz)
        iterm[q] = lax.dot_general(
            gg[...], wts[lax.div(q, NX), lax.rem(q, NX)].reshape(cols, cols), NT, preferred_element_type=F32
        ).astype(BF)

    made = set()

    def need_iterm(block):
        if block % nz not in made:
            made.add(block % nz)
            make_iterm(block)

    def i_chunk(block, ch):
        return iterm.at[wrap(z + block, nz), pl.ds(span * ch, span), :]

    def hidden_relay(t):
        yield from until("v", t)
        gate_gradient()
        flags.add("g")
        ready = []
        flying = {}

        def mature(ch, sign, limit, k):
            kids = children_of(RING, k, limit)
            return max((mature(ch, sign, limit, kid) + hop_time(kid - k) for kid in kids), default=0.3 * ch)

        def depth(ch, k):
            return 0 if k == 0 else depth(ch, RING[k]) + 1

        for ch in range(CHUNKS):
            for sign, limit in limits(ch):
                for k in range(limit + 1):
                    ready.append((mature(ch, sign, limit, k), -depth(ch, k), len(ready), ch, sign, limit, k))
        ends = {}
        start = t + 0.5
        for when, _, _, ch, sign, limit, k in sorted(ready):
            yield start + when
            need_iterm(sign * k)
            here = pl.ds(span * ch, span)
            side = (1 - sign) // 2
            q = wrap(z + sign * k, nz)
            kids = children_of(RING, k, limit)
            if kids:
                total = iterm[q, here, :].astype(F32) if k or ch not in ends else gin[here, :]
                for kid in kids:
                    flying[ch, sign, kid].wait_recv()
                    total = total + ri[side, kid - 1, here, :].astype(F32)
                if k:
                    iterm[q, here, :] = total.astype(BF)
                elif ch in ends:
                    gh_out[here, :] = total.astype(BF)
                else:
                    gin[here, :] = total
                    ends[ch] = True
            if k:
                parent = RING[k]
                flying[ch, sign, k] = send(i_chunk(sign * k, ch), ri.at[side, k - 1, here, :], zdev(sign * (k - parent)))

    def plane_reduce(slices, half, bufs, t, small, large, finish):
        piece, row, col = slices
        rb, rp = bufs
        if half == 0:
            bundle = lambda p: row(p, half)
            line = lambda p: piece(y, p, half)
            pos, near, pos2, near2, n1, n2 = y, ydev, x, xdev, NY, NX
        else:
            bundle = lambda p: col(p, half)
            line = lambda p: piece(p, x, half)
            pos, near, pos2, near2, n1, n2 = x, xdev, y, ydev, NX, NY
        for stage, (at, p0, nr, n, rbuf, dt) in enumerate(
            ((bundle, pos, near, n1, rb, large), (line, pos2, near2, n2, rp, small))
        ):
            out = [send(at(wrap(p0 + k, n)), rbuf.at[k - 1], nr(k)) for k in (2, 1, 3)]
            t += dt
            yield t
            for cp in out:
                cp.wait_recv()
            mine = at(p0)
            total = mine[...].astype(F32)
            for k in range(3):
                total = total + rbuf[k].astype(F32)
            if stage == 0:
                mine[...] = total.astype(BF)
            else:
                finish(total)

    def ts_piece(yy, xx, half):
        return tsum.at[pl.ds(4 * half, 4), lax.rem(yy, 2), xx, :, hi(yy)]

    def ts_row(yy, half):
        return tsum.at[pl.ds(4 * half, 4), lax.rem(yy, 2), :, :, hi(yy)]

    def ts_col(xx, half):
        return tsum.at[pl.ds(4 * half, 4), :, xx]

    def g_src(j):
        jl = j - 8 * (1 - c)
        return tfin.at[jl]

    def g_src_fixed(j):
        return tfin.at[0] if isinstance(j, int) else g_src(j)

    def g_dst(j):
        return gvals.at[j, ylow, x, :, hi(y)]

    g_slices = t_slices(gvals)

    def t_half(half):
        yield T0
        if half == 0:
            t_swap[0].wait_recv()
        here = pl.ds(4 * half, 4)
        for jl in range(4 * half, 4 * half + 4):
            part = jnp.dot(pair_t[jl], pair_mg[...], preferred_element_type=F32)
            tsum[jl] = part.astype(BF).reshape(2, NX, 16, cols)

        def finish(total):
            tfin[here] = total.astype(BF)

        yield from plane_reduce(
            (ts_piece, ts_row, ts_col), half, (tr_row if half == 0 else tr_col, tr_piece.at[half]),
            T0, 4.0, 6.0, finish,
        )

    def t_path():
        yield from until("h", 18.5)
        value_terms()
        yield from both(t_half)
        done = tile_exchange(g_src_fixed, g_dst, lambda j: j)
        yield T0 + 18.0
        done()
        yield from both(lambda half: plane_gather(g_slices, half, T0 + 18.0, 3.5, 5.5, 2.0))

    def ps_piece(yy, xx, half):
        return psum.at[yy, xx, pl.ds(128 * half, 128), :]

    def ps_row(yy, half):
        return psum.at[yy, :, pl.ds(128 * half, 128), :]

    def ps_col(xx, half):
        return psum.at[:, xx, pl.ds(128 * half, 128), :]

    def p_half(half):
        here = pl.ds(128 * half, 128)
        yield from until("g", 25.5 + half)
        yield 28.2 + half
        for q in range(nz):
            pterm[q // NX, q % NX, here, :] = jnp.dot(ggt[here, :], hid[q], preferred_element_type=F32).astype(BF)
        swap = send(
            pterm.at[:, :, here, pl.ds(mult(128 * oc, 128), 128)], pr0.at[half], partner
        )
        yield 32.0 + half
        swap.wait_recv()
        own = pterm[:, :, here, pl.ds(mult(128 * c, 128), 128)]
        psum[:, :, here, :] = (own.astype(F32) + pr0[half].astype(F32)).astype(BF)

        def finish(total):
            gg_out[:, pl.ds(128 * half, 128)] = total.T

        yield from plane_reduce(
            (ps_piece, ps_row, ps_col), half, (pr_bundle.at[half], pr_piece.at[half]), 32.0 + half, 4.5, 8.5, finish
        )

    def aff_path():
        yield from until("g", 26.0)
        yield 30.0
        lane = jnp.bitwise_and(idx[...], 127)
        chunk = lax.shift_right_logical(idx[...], 7)
        acc = jnp.zeros((rows_blk, 128), F32)
        for j in range(nz):
            part = lax.dot_general(mg[...], vals[j].reshape(rows_blk, cols), NT, preferred_element_type=F32)
            got = jnp.take_along_axis(part, lane, axis=1, mode="promise_in_bounds")
            acc = jnp.where(chunk == j, got, acc)
        acc_t = acc.T
        for i in range(nz):
            affp[i] = acc_t[2 * i : 2 * i + 2, :]
        cps = [send(affp.at[wrap(z + k, nz)], affr.at[k], zdev(k)) for k in range(1, nz)]
        yield 38.5
        total = affp[z]
        for k in range(1, nz):
            cps[k - 1].wait_recv()
            total = total + affr[k]
        affall[z] = total
        cps = [send(affall.at[z], affall.at[z], zdev(k)) for k in range(1, nz)]
        yield 46.5
        for cp in cps:
            cp.wait_recv()
        for i in range(nz):
            afft[2 * i : 2 * i + 2, :] = affall[i]
        weights = wgt[...]
        aff = afft[...]
        gs_out[...] = weights * (aff - jnp.sum(weights * aff, axis=0, keepdims=True))

    run_streams(
        [v_path(), hid_relay(0.0), w_path(), spread_path(), t_path(), hidden_relay(25.2), p_half(0), p_half(1), aff_path()]
    )

    for cp in sent:
        cp.wait_send()


def write_out(nz, bo_in, gh_in, gg_in, gvals_in, gs_in, bo_out, gh_out, gg_out, gv_out, gs_out, wide, sem):
    rows, cols = bo_in.shape
    z = lax.axis_index("table")
    small = ((bo_in, bo_out), (gh_in, gh_out), (gg_in, gg_out), (gs_in, gs_out))
    copies = [pltpu.make_async_copy(src, dst, sem.at[nz + i]) for i, (src, dst) in enumerate(small)]
    for cp in copies:
        cp.start()
    for j in range(nz):
        wide[j] = gvals_in[j].reshape(rows, cols).astype(F32)
        q = wrap(z - j, nz)
        cp = pltpu.make_async_copy(wide.at[j], gv_out.at[:, pl.ds(mult(q * cols, cols), cols)], sem.at[j])
        cp.start()
        copies.append(cp)
    for cp in copies:
        cp.wait()


def layer(nz, hidden_in, gate_weight, values, pick_rows, pick_scores, grad_out):
    rows, cols = hidden_in.shape
    vm = pltpu.VMEM
    scratch = [
        vm((nz, rows, cols), BF),
        vm((NY, NX, 2, rows, cols), BF),
        vm((nz, 2, NX, 16, cols), BF),
        vm((rows, nz * rows), BF),
        vm((nz, rows, rows), BF),
        vm((rows, cols), BF),
        vm((rows, cols), F32),
        vm((rows, cols), BF),
        vm((rows, cols), BF),
        vm((cols, rows), BF),
        vm((rows, 128), F32),
        vm((32, rows), jnp.int32),
        vm((32, rows), jnp.int32),
        vm((32, rows), F32),
        vm((rows, 128), jnp.int32),
        vm((NY, NX, cols, cols), BF),
        vm((2, NY, NX, 128, 128), BF),
        vm((NY, NX, cols, 128), BF),
        vm((2, 3, 4, 128, 128), BF),
        vm((2, 3, 128, 128), BF),
        vm((8, rows, 2 * rows), BF),
        vm((2 * rows, cols), BF),
        vm((8, 2, NX, 16, cols), BF),
        vm((3, 4, NX, 16, 128), BF),
        vm((3, 4, 2, 16, cols), BF),
        vm((2, 3, 4, 16, 128), BF),
        vm((8, 16, 128), BF),
        vm((nz, rows, cols), BF),
        vm((2, nz // 2, rows, cols), BF),
        vm((nz, 2, 128), F32),
        vm((nz, 2, 128), F32),
        vm((nz, 2, 128), F32),
        vm((32, 128), F32),
        pltpu.SemaphoreType.DMA((N_COPIES,)),
        pltpu.SemaphoreType.DMA((N_COPIES,)),
        pltpu.SemaphoreType.DMA((N_LOCAL,)),
        pltpu.SemaphoreType.REGULAR((2,)),
    ]
    hbm = pl.BlockSpec(memory_space=pl.ANY)
    vmem = pl.BlockSpec(memory_space=pltpu.VMEM)
    arrays = (hidden_in, gate_weight, values, pick_rows.T, pick_scores.T, grad_out)
    arrays = [pltpu.with_memory_space_constraint(a, pltpu.HBM) for a in arrays]
    parts = pl.pallas_call(
        functools.partial(body, nz),
        out_shape=(
            jax.ShapeDtypeStruct((rows, cols), BF),
            jax.ShapeDtypeStruct((rows, cols), BF),
            jax.ShapeDtypeStruct((rows, cols), F32),
            jax.ShapeDtypeStruct((nz, 2, NX, 16, cols), BF),
            jax.ShapeDtypeStruct((32, rows), F32),
        ),
        in_specs=[pl.BlockSpec(memory_space=pltpu.HBM)] * 6,
        out_specs=(vmem, vmem, vmem, hbm, vmem),
        scratch_shapes=scratch,
        compiler_params=pltpu.CompilerParams(
            collective_id=0, has_side_effects=True, vmem_limit_bytes=32 * 1024 * 1024
        ),
    )(*arrays)
    bo, gh, gg, gv, gs = pl.pallas_call(
        functools.partial(write_out, nz),
        out_shape=(
            jax.ShapeDtypeStruct((rows, cols), BF),
            jax.ShapeDtypeStruct((rows, cols), BF),
            jax.ShapeDtypeStruct((rows, cols), F32),
            jax.ShapeDtypeStruct((rows, nz * cols), F32),
            jax.ShapeDtypeStruct((32, rows), F32),
        ),
        in_specs=[vmem] * 5,
        out_specs=(hbm,) * 5,
        scratch_shapes=[pltpu.VMEM((nz, rows, cols), F32), pltpu.SemaphoreType.DMA((nz + 4,))],
        compiler_params=pltpu.CompilerParams(vmem_limit_bytes=8 * 1024 * 1024),
    )(*parts)
    return bo, gh, gg, gv, gs.T


def solution(mesh):
    nz = mesh.shape["table"]
    return jax.shard_map(
        functools.partial(layer, nz),
        mesh=mesh,
        in_specs=(
            P("dp", "table"),
            P("dp", "table"),
            P("table", None),
            P("dp", None),
            P("dp", None),
            P("dp", "table"),
        ),
        out_specs=(
            P("dp", "table"),
            P("dp", "table"),
            P("dp", "table"),
            P("table", None),
            P("dp", None),
        ),
        check_vma=False,
    )
```

```python
import functools
import heapq

import jax
import jax.numpy as jnp
from jax import lax
from jax.experimental import pallas as pl
from jax.experimental.pallas import tpu as pltpu
from jax.sharding import PartitionSpec as P

MESH_ID = pl.DeviceIdType.MESH
F32 = jnp.float32
BF = jnp.bfloat16
NX = 4
NY = 4
CHUNKS = 4
N_COPIES = 320
N_LOCAL = 16
T0 = 22.0
NT = (((1,), (1,)), ((), ()))
RELAY = {1: 0, 2: 0, 3: 2, 4: 2, 5: 4, 6: 4, 7: 6, 8: 6}
RING = {k: k - 1 for k in range(1, 9)}


def hop_time(links):
    return 3.4 + 1.0 * (links - 1)


def children_of(parents, node, limit):
    return sorted((k for k, p in parents.items() if p == node and k <= limit), reverse=True)


def wrap(value, size):
    return lax.rem(value + size, size)


def mult(value, unit):
    return pl.multiple_of(value, unit)


def run_streams(streams):
    heap = []
    for order, stream in enumerate(streams):
        heapq.heappush(heap, (0.0, order, stream))
    while heap:
        when, order, stream = heapq.heappop(heap)
        try:
            due = next(stream)
        except StopIteration:
            continue
        heapq.heappush(heap, (due, order, stream))


def body(
    nz,
    hid_in, w_in, val_in, rows_in, score_in, go_in,
    bo_out, gh_out, gg_out, gvals, gs_out,
    hid, wts, vals, spread, spread_t, go, gin, silu, lift, mg, gg, ggt, pad_a, picks, rel_t, wgt, idx,
    pterm, pr0, psum, pr_bundle, pr_piece,
    pair_t, pair_mg, tsum, tr_row, tr_col, tr_piece, tfin,
    iterm, ri, affp, affr, affall, afft,
    send_sem, recv_sem, local_sem, know,
):
    rows_blk = hid_in.shape[0]
    cols = hid_in.shape[1]
    b = lax.axis_index("dp")
    z = lax.axis_index("table")
    c = lax.rem(b, 2)
    x = lax.rem(lax.div(b, 2), NX)
    y = lax.div(b, 2 * NX)
    s = 1 - 2 * c
    oc = 1 - c

    def dev(yy, xx, cc):
        return ((yy * NX + xx) * 2 + cc, z)

    def zdev(delta):
        return (b, wrap(z + delta, nz))

    def xdev(delta):
        return dev(y, wrap(x + delta, NX), c)

    def ydev(delta):
        return dev(wrap(y + delta, NY), x, c)

    partner = dev(y, x, oc)

    barrier = pltpu.get_barrier_semaphore()
    peers = [zdev(k) for k in (1, -1, 2, -2)] + [xdev(k) for k in (1, 2, 3)] + [ydev(k) for k in (1, 2, 3)]
    peers.append(partner)
    for peer in peers:
        pl.semaphore_signal(barrier, inc=1, device_id=peer, device_id_type=MESH_ID)

    local_count = [0]
    copy_count = [0]
    sent = []

    def lcopy(src, dst):
        i = local_count[0]
        local_count[0] += 1
        cp = pltpu.make_async_copy(src, dst, local_sem.at[i])
        cp.start()
        return cp

    def send(src, dst, peer):
        i = copy_count[0]
        copy_count[0] += 1
        cp = pltpu.make_async_remote_copy(
            src_ref=src, dst_ref=dst, send_sem=send_sem.at[i], recv_sem=recv_sem.at[i],
            device_id=peer, device_id_type=MESH_ID,
        )
        cp.start()
        sent.append(cp)
        return cp

    own_h = lcopy(hid_in, hid.at[z])
    own_w = lcopy(w_in, wts.at[y, x, c])
    own_rows = lcopy(rows_in, picks)
    own_scores = lcopy(score_in, wgt)
    own_g = lcopy(go_in, go)

    ylow = lax.rem(y, 2)
    yhigh = lax.div(y, 2)

    total_rows = nz * rows_blk

    def relative(row_f):
        shifted = row_f.astype(jnp.int32) + (total_rows - rows_blk * z)
        return jnp.where(shifted >= total_rows, shifted - total_rows, shifted)

    def spread_block(i, carry):
        ids = lax.broadcasted_iota(jnp.int32, (rows_blk, rows_blk), 0) + i * rows_blk
        acc = jnp.zeros((rows_blk, rows_blk), F32)
        for k in range(32):
            acc = jnp.where(rel_t[k : k + 1, :] == ids, afft[k : k + 1, :], acc)
        spread_t[i] = acc.astype(BF)
        spread[:, pl.ds(mult(i * rows_blk, rows_blk), rows_blk)] = acc.T.astype(BF)
        return carry

    own_h.wait()
    pl.semaphore_wait(barrier, len(peers))

    def w_piece(yy, xx, cc, half):
        return wts.at[yy, xx, cc, :, pl.ds(128 * half, 128)]

    def w_row(yy, cc, half):
        return wts.at[yy, :, cc, :, pl.ds(128 * half, 128)]

    def w_col(xx, cc, half):
        return wts.at[:, xx, cc, :, pl.ds(128 * half, 128)]

    def jset(cc, half):
        return pl.ds(8 * (1 - cc) + 4 * half, 4)

    def hi(yy):
        return pl.ds(mult(128 * lax.div(yy, 2), 128), 128)

    def t_slices(buf):
        def piece(yy, xx, cc, half):
            return buf.at[jset(cc, half), lax.rem(yy, 2), xx, :, hi(yy)]

        def row(yy, cc, half):
            return buf.at[jset(cc, half), lax.rem(yy, 2), :, :, hi(yy)]

        def col(xx, cc, half):
            return buf.at[jset(cc, half), :, xx]

        return piece, row, col

    flags = set()

    def until(name, t):
        while name not in flags:
            yield t
            t += 0.5

    def both(make):
        live = [make(half) for half in (0, 1)]
        while live:
            due = None
            for part in list(live):
                try:
                    due = next(part)
                except StopIteration:
                    live.remove(part)
            if live:
                yield due

    def plane_gather(slices, half, t, first_step, second_step, third_step):
        piece, row, col = slices
        if half == 0:
            line = lambda p: piece(y, p, c, half)
            bundle = lambda p: row(p, c, half)
            pos, near, pos2, near2, n1, n2 = x, xdev, y, ydev, NX, NY
        else:
            line = lambda p: piece(p, x, c, half)
            bundle = lambda p: col(p, c, half)
            pos, near, pos2, near2, n1, n2 = y, ydev, x, xdev, NY, NX
        out = [send(line(pos), line(pos), near(k)) for k in (2, 1, 3)]
        t += first_step
        yield t
        for cp in out:
            cp.wait_recv()
        out = [send(bundle(pos2), bundle(pos2), near2(k)) for k in (2, 1, 3)]
        swap = [send(bundle(pos2), bundle(pos2), partner)]
        t += second_step
        yield t
        for k, cp in ((1, out[1]), (3, out[2]), (2, out[0])):
            cp.wait_recv()
            p = wrap(pos2 - k, n2)
            swap.append(send(bundle(p), bundle(p), partner))
        t += third_step
        yield t
        for cp in swap:
            cp.wait_recv()

    pending = []
    first = [True]

    def accumulate(block):
        q = wrap(z + block, nz)
        part = jnp.dot(
            hid[q], wts[lax.div(q, NX), lax.rem(q, NX)].reshape(cols, cols), preferred_element_type=F32
        )
        if first[0]:
            gin[...] = part
            first[0] = False
        else:
            gin[...] += part

    arrived = {}

    def block_here(block, parts):
        arrived[block] = arrived.get(block, 0) + parts
        if arrived[block] == CHUNKS:
            if "w" in flags:
                accumulate(block)
            else:
                pending.append(block)

    span = rows_blk // CHUNKS

    def hid_chunk(block, ch):
        return hid.at[wrap(z + block, nz), pl.ds(span * ch, span), :]

    def limits(ch):
        up = nz // 2 if ch % 2 == 0 else nz // 2 - 1
        return ((1, up), (-1, nz - 1 - up))

    def hid_relay(t):
        waiting = []

        def pass_on(ch, sign, limit, k, now):
            at = hid_chunk(-sign * k, ch)
            for child in children_of(RELAY, k, limit):
                cp = send(at, at, zdev(sign * (child - k)))
                leaf = 0.0 if children_of(RELAY, child, limit) else 2.0
                heapq.heappush(waiting, (now + hop_time(child - k) + leaf, len(sent), ch, sign, limit, child, cp))

        for ch in range(CHUNKS):
            for sign, limit in limits(ch):
                pass_on(ch, sign, limit, 0, t + 0.3 * ch)
        block_here(0, CHUNKS)
        while waiting:
            yield waiting[0][0]
            now, _, ch, sign, limit, k, cp = heapq.heappop(waiting)
            cp.wait_recv()
            pass_on(ch, sign, limit, k, now)
            block_here((-sign * k) % nz, 1)
        yield from until("w", now)
        flags.add("h")

    def tile_exchange(make_src, make_dst, toward):
        cps = []
        for i in range(1, nz // 2):
            j = jnp.where(c == 0, nz - i, i)
            cps.append(send(make_src(j), make_dst(j), (b, wrap(z + toward(j), nz))))
        half = nz // 2
        i = copy_count[0]
        copy_count[0] += 1
        last = pltpu.make_async_remote_copy(
            src_ref=make_src(half), dst_ref=make_dst(half), send_sem=send_sem.at[i], recv_sem=recv_sem.at[i],
            device_id=zdev(half), device_id_type=MESH_ID,
        )
        i = local_count[0]
        local_count[0] += 1
        own = pltpu.make_async_copy(make_src(0), make_dst(0), local_sem.at[i])

        @pl.when(c == 0)
        def _():
            last.start()

        @pl.when(c == 1)
        def _():
            own.start()

        def finish():
            for cp in cps:
                cp.wait_recv()

            @pl.when(c == 0)
            def _():
                last.wait()

            @pl.when(c == 1)
            def _():
                own.wait()

        return finish

    v_slices = t_slices(vals)
    tile_rows = lax.rem(y, 2) * NX + x

    def val_src(j):
        zd = wrap(z - j, nz)
        return val_in.at[pl.ds(mult(16 * tile_rows, 16), 16), pl.ds(mult(cols * zd + 128 * yhigh, 128), 128)]

    def val_dst(j):
        return vals.at[j, ylow, x, :, hi(y)]

    def both(make):
        parts = [make(half) for half in (0, 1)]
        live = list(parts)
        while live:
            due = None
            for part in list(live):
                try:
                    due = next(part)
                except StopIteration:
                    live.remove(part)
            if live:
                yield due

    def v_path():
        for stage, reach in enumerate((2, 4)):
            for sign in (1, -1):
                pl.semaphore_signal(know.at[stage], inc=1, device_id=zdev(sign * reach), device_id_type=MESH_ID)
            yield (1.5, 4.0)[stage]
            pl.semaphore_wait(know.at[stage], 2)
        finish = tile_exchange(val_src, val_dst, lambda j: nz - j)
        yield 13.5
        finish()
        yield from both(lambda half: plane_gather(v_slices, half, 13.5, 3.5, 6.0, 2.0))
        flags.add("v")

    w_slices = (w_piece, w_row, w_col)

    def spread_path():
        yield 0.2
        pad_a[...] = jnp.zeros_like(pad_a)
        own_rows.wait()
        own_scores.wait()
        pad_a[0:32, :] = picks[...].astype(F32)
        idx[...] = relative(pad_a[...].T)
        rel_t[...] = relative(pad_a[0:32, :])
        scores = wgt[...]
        expo = jnp.exp(scores - jnp.max(scores, axis=0, keepdims=True))
        wgt[...] = expo / jnp.sum(expo, axis=0, keepdims=True)
        afft[...] = wgt[...].astype(BF).astype(F32)
        lax.fori_loop(0, nz, spread_block, 0)
        own_g.wait()
        pair_t[:, :, 0:128] = spread_t[pl.ds(8 * (1 - c), 8)]
        share = send(spread_t.at[pl.ds(8 * (1 - oc), 8)], pair_t.at[:, :, pl.ds(128, 128)], partner)
        yield 8.0
        share.wait_recv()

    def w_path():
        own_w.wait()
        yield from both(lambda half: plane_gather(w_slices, half, 0.0, 3.5, 9.0, 2.0))
        flags.add("w")
        for block in pending:
            accumulate(block)
        pending.clear()

    def gate_parts():
        gate = gin[...]
        sig = jax.nn.sigmoid(gate)
        return gate, sig, go[...].astype(F32)

    t_swap = []

    def value_terms():
        gate, sig, upstream = gate_parts()
        mg[...] = (upstream * (gate * sig)).astype(BF)
        pair_mg[0:128, :] = mg[...]
        t_swap.append(send(mg, pair_mg.at[pl.ds(128, 128)], partner))
        silu[...] = gate * sig
        lift[...] = upstream * (sig * (1.0 + gate * (1.0 - sig)))

    def gate_gradient():
        memory_read = jnp.dot(spread[...], vals[...].reshape(total_rows, cols), preferred_element_type=F32)
        slope = (memory_read * lift[...]).astype(BF)
        gg[...] = slope
        bo_out[...] = (memory_read * silu[...]).astype(BF)
        ggt[...] = slope.astype(F32).T.astype(BF)

    def make_iterm(block):
        q = wrap(z + block, nz)
        iterm[q] = lax.dot_general(
            gg[...], wts[lax.div(q, NX), lax.rem(q, NX)].reshape(cols, cols), NT, preferred_element_type=F32
        ).astype(BF)

    made = set()

    def need_iterm(block):
        if block % nz not in made:
            made.add(block % nz)
            make_iterm(block)

    def i_chunk(block, ch):
        return iterm.at[wrap(z + block, nz), pl.ds(span * ch, span), :]

    def hidden_relay(t):
        yield from until("v", t)
        gate_gradient()
        flags.add("g")
        ready = []
        flying = {}

        def mature(ch, sign, limit, k):
            kids = children_of(RING, k, limit)
            return max((mature(ch, sign, limit, kid) + hop_time(kid - k) for kid in kids), default=0.3 * ch)

        def depth(ch, k):
            return 0 if k == 0 else depth(ch, RING[k]) + 1

        for ch in range(CHUNKS):
            for sign, limit in limits(ch):
                for k in range(limit + 1):
                    ready.append((mature(ch, sign, limit, k), -depth(ch, k), len(ready), ch, sign, limit, k))
        ends = {}
        start = t + 0.5
        for when, _, _, ch, sign, limit, k in sorted(ready):
            yield start + when
            need_iterm(sign * k)
            here = pl.ds(span * ch, span)
            side = (1 - sign) // 2
            q = wrap(z + sign * k, nz)
            kids = children_of(RING, k, limit)
            if kids:
                total = iterm[q, here, :].astype(F32) if k or ch not in ends else gin[here, :]
                for kid in kids:
                    flying[ch, sign, kid].wait_recv()
                    total = total + ri[side, kid - 1, here, :].astype(F32)
                if k:
                    iterm[q, here, :] = total.astype(BF)
                elif ch in ends:
                    gh_out[here, :] = total.astype(BF)
                else:
                    gin[here, :] = total
                    ends[ch] = True
            if k:
                parent = RING[k]
                flying[ch, sign, k] = send(i_chunk(sign * k, ch), ri.at[side, k - 1, here, :], zdev(sign * (k - parent)))

    def plane_reduce(slices, half, bufs, t, small, large, finish):
        piece, row, col = slices
        rb, rp = bufs
        if half == 0:
            bundle = lambda p: row(p, half)
            line = lambda p: piece(y, p, half)
            pos, near, pos2, near2, n1, n2 = y, ydev, x, xdev, NY, NX
        else:
            bundle = lambda p: col(p, half)
            line = lambda p: piece(p, x, half)
            pos, near, pos2, near2, n1, n2 = x, xdev, y, ydev, NX, NY
        for stage, (at, p0, nr, n, rbuf, dt) in enumerate(
            ((bundle, pos, near, n1, rb, large), (line, pos2, near2, n2, rp, small))
        ):
            out = [send(at(wrap(p0 + k, n)), rbuf.at[k - 1], nr(k)) for k in (2, 1, 3)]
            t += dt
            yield t
            for cp in out:
                cp.wait_recv()
            mine = at(p0)
            total = mine[...].astype(F32)
            for k in range(3):
                total = total + rbuf[k].astype(F32)
            if stage == 0:
                mine[...] = total.astype(BF)
            else:
                finish(total)

    def ts_piece(yy, xx, half):
        return tsum.at[pl.ds(4 * half, 4), lax.rem(yy, 2), xx, :, hi(yy)]

    def ts_row(yy, half):
        return tsum.at[pl.ds(4 * half, 4), lax.rem(yy, 2), :, :, hi(yy)]

    def ts_col(xx, half):
        return tsum.at[pl.ds(4 * half, 4), :, xx]

    def g_src(j):
        jl = j - 8 * (1 - c)
        return tfin.at[jl]

    def g_src_fixed(j):
        return tfin.at[0] if isinstance(j, int) else g_src(j)

    def g_dst(j):
        return gvals.at[j, ylow, x, :, hi(y)]

    g_slices = t_slices(gvals)

    def t_half(half):
        yield T0
        if half == 0:
            t_swap[0].wait_recv()
        here = pl.ds(4 * half, 4)
        for jl in range(4 * half, 4 * half + 4):
            part = jnp.dot(pair_t[jl], pair_mg[...], preferred_element_type=F32)
            tsum[jl] = part.astype(BF).reshape(2, NX, 16, cols)

        def finish(total):
            tfin[here] = total.astype(BF)

        yield from plane_reduce(
            (ts_piece, ts_row, ts_col), half, (tr_row if half == 0 else tr_col, tr_piece.at[half]),
            T0, 4.0, 6.0, finish,
        )

    def t_path():
        yield from until("h", 18.5)
        value_terms()
        yield from both(t_half)
        done = tile_exchange(g_src_fixed, g_dst, lambda j: j)
        yield T0 + 18.0
        done()
        yield from both(lambda half: plane_gather(g_slices, half, T0 + 18.0, 3.5, 5.5, 2.0))

    def ps_piece(yy, xx, half):
        return psum.at[yy, xx, pl.ds(128 * half, 128), :]

    def ps_row(yy, half):
        return psum.at[yy, :, pl.ds(128 * half, 128), :]

    def ps_col(xx, half):
        return psum.at[:, xx, pl.ds(128 * half, 128), :]

    def p_half(half):
        here = pl.ds(128 * half, 128)
        yield from until("g", 25.5 + half)
        yield 28.2 + half
        for q in range(nz):
            pterm[q // NX, q % NX, here, :] = jnp.dot(ggt[here, :], hid[q], preferred_element_type=F32).astype(BF)
        swap = send(
            pterm.at[:, :, here, pl.ds(mult(128 * oc, 128), 128)], pr0.at[half], partner
        )
        yield 32.0 + half
        swap.wait_recv()
        own = pterm[:, :, here, pl.ds(mult(128 * c, 128), 128)]
        psum[:, :, here, :] = (own.astype(F32) + pr0[half].astype(F32)).astype(BF)

        def finish(total):
            gg_out[:, pl.ds(128 * half, 128)] = total.T

        yield from plane_reduce(
            (ps_piece, ps_row, ps_col), half, (pr_bundle.at[half], pr_piece.at[half]), 32.0 + half, 4.5, 8.5, finish
        )

    def aff_path():
        yield from until("g", 26.0)
        yield 30.0
        lane = jnp.bitwise_and(idx[...], 127)
        chunk = lax.shift_right_logical(idx[...], 7)
        acc = jnp.zeros((rows_blk, 128), F32)
        for j in range(nz):
            part = lax.dot_general(mg[...], vals[j].reshape(rows_blk, cols), NT, preferred_element_type=F32)
            got = jnp.take_along_axis(part, lane, axis=1, mode="promise_in_bounds")
            acc = jnp.where(chunk == j, got, acc)
        acc_t = acc.T
        for i in range(nz):
            affp[i] = acc_t[2 * i : 2 * i + 2, :]
        cps = [send(affp.at[wrap(z + k, nz)], affr.at[k], zdev(k)) for k in range(1, nz)]
        yield 38.5
        total = affp[z]
        for k in range(1, nz):
            cps[k - 1].wait_recv()
            total = total + affr[k]
        affall[z] = total
        cps = [send(affall.at[z], affall.at[z], zdev(k)) for k in range(1, nz)]
        yield 46.5
        for cp in cps:
            cp.wait_recv()
        for i in range(nz):
            afft[2 * i : 2 * i + 2, :] = affall[i]
        weights = wgt[...]
        aff = afft[...]
        gs_out[...] = weights * (aff - jnp.sum(weights * aff, axis=0, keepdims=True))

    run_streams(
        [v_path(), hid_relay(0.0), w_path(), spread_path(), t_path(), hidden_relay(25.2), p_half(0), p_half(1), aff_path()]
    )

    for cp in sent:
        cp.wait_send()


def write_out(nz, bo_in, gh_in, gg_in, gvals_in, gs_in, bo_out, gh_out, gg_out, gv_out, gs_out, wide, sem):
    rows, cols = bo_in.shape
    z = lax.axis_index("table")
    small = ((bo_in, bo_out), (gh_in, gh_out), (gg_in, gg_out), (gs_in, gs_out))
    copies = [pltpu.make_async_copy(src, dst, sem.at[nz + i]) for i, (src, dst) in enumerate(small)]
    for cp in copies:
        cp.start()
    for j in range(nz):
        wide[j] = gvals_in[j].reshape(rows, cols).astype(F32)
        q = wrap(z - j, nz)
        cp = pltpu.make_async_copy(wide.at[j], gv_out.at[:, pl.ds(mult(q * cols, cols), cols)], sem.at[j])
        cp.start()
        copies.append(cp)
    for cp in copies:
        cp.wait()


def layer(nz, hidden_in, gate_weight, values, pick_rows, pick_scores, grad_out):
    rows, cols = hidden_in.shape
    vm = pltpu.VMEM
    scratch = [
        vm((nz, rows, cols), BF),
        vm((NY, NX, 2, rows, cols), BF),
        vm((nz, 2, NX, 16, cols), BF),
        vm((rows, nz * rows), BF),
        vm((nz, rows, rows), BF),
        vm((rows, cols), BF),
        vm((rows, cols), F32),
        vm((rows, cols), F32),
        vm((rows, cols), F32),
        vm((rows, cols), BF),
        vm((rows, cols), BF),
        vm((cols, rows), BF),
        vm((rows, 128), F32),
        vm((32, rows), jnp.int32),
        vm((32, rows), jnp.int32),
        vm((32, rows), F32),
        vm((rows, 128), jnp.int32),
        vm((NY, NX, cols, cols), BF),
        vm((2, NY, NX, 128, 128), BF),
        vm((NY, NX, cols, 128), BF),
        vm((2, 3, 4, 128, 128), BF),
        vm((2, 3, 128, 128), BF),
        vm((8, rows, 2 * rows), BF),
        vm((2 * rows, cols), BF),
        vm((8, 2, NX, 16, cols), BF),
        vm((3, 4, NX, 16, 128), BF),
        vm((3, 4, 2, 16, cols), BF),
        vm((2, 3, 4, 16, 128), BF),
        vm((8, 16, 128), BF),
        vm((nz, rows, cols), BF),
        vm((2, nz // 2, rows, cols), BF),
        vm((nz, 2, 128), F32),
        vm((nz, 2, 128), F32),
        vm((nz, 2, 128), F32),
        vm((32, 128), F32),
        pltpu.SemaphoreType.DMA((N_COPIES,)),
        pltpu.SemaphoreType.DMA((N_COPIES,)),
        pltpu.SemaphoreType.DMA((N_LOCAL,)),
        pltpu.SemaphoreType.REGULAR((2,)),
    ]
    hbm = pl.BlockSpec(memory_space=pl.ANY)
    vmem = pl.BlockSpec(memory_space=pltpu.VMEM)
    arrays = (hidden_in, gate_weight, values, pick_rows.T, pick_scores.T, grad_out)
    arrays = [pltpu.with_memory_space_constraint(a, pltpu.HBM) for a in arrays]
    parts = pl.pallas_call(
        functools.partial(body, nz),
        out_shape=(
            jax.ShapeDtypeStruct((rows, cols), BF),
            jax.ShapeDtypeStruct((rows, cols), BF),
            jax.ShapeDtypeStruct((rows, cols), F32),
            jax.ShapeDtypeStruct((nz, 2, NX, 16, cols), BF),
            jax.ShapeDtypeStruct((32, rows), F32),
        ),
        in_specs=[pl.BlockSpec(memory_space=pltpu.HBM)] * 6,
        out_specs=(vmem, vmem, vmem, hbm, vmem),
        scratch_shapes=scratch,
        compiler_params=pltpu.CompilerParams(
            collective_id=0, has_side_effects=True, vmem_limit_bytes=32 * 1024 * 1024
        ),
    )(*arrays)
    bo, gh, gg, gv, gs = pl.pallas_call(
        functools.partial(write_out, nz),
        out_shape=(
            jax.ShapeDtypeStruct((rows, cols), BF),
            jax.ShapeDtypeStruct((rows, cols), BF),
            jax.ShapeDtypeStruct((rows, cols), F32),
            jax.ShapeDtypeStruct((rows, nz * cols), F32),
            jax.ShapeDtypeStruct((32, rows), F32),
        ),
        in_specs=[vmem] * 5,
        out_specs=(hbm,) * 5,
        scratch_shapes=[pltpu.VMEM((nz, rows, cols), F32), pltpu.SemaphoreType.DMA((nz + 4,))],
        compiler_params=pltpu.CompilerParams(vmem_limit_bytes=8 * 1024 * 1024),
    )(*parts)
    return bo, gh, gg, gv, gs.T


def solution(mesh):
    nz = mesh.shape["table"]
    return jax.shard_map(
        functools.partial(layer, nz),
        mesh=mesh,
        in_specs=(
            P("dp", "table"),
            P("dp", "table"),
            P("table", None),
            P("dp", None),
            P("dp", None),
            P("dp", "table"),
        ),
        out_specs=(
            P("dp", "table"),
            P("dp", "table"),
            P("dp", "table"),
            P("table", None),
            P("dp", None),
        ),
        check_vma=False,
    )
```
